32 devices in a mesh: tokens: 4 (over y, x), tensor: 8 (over z, core).
Axes of the slice: x: 2, y: 2, z: 4, core: 2. Of those that a mesh axis runs over, the one named last changes fastest.
Arguments:
- codes: int32 [2, 1536, 5120], P(None, ('tokens', 'tensor')), may hold values from 0 to 254, as said below
- scales: int32 [2, 1536, 160], P(None, ('tokens', 'tensor')), may hold values from 119 to 122
- w_qkv: bfloat16 [5120, 15360], P(None, 'tensor'), may hold values from -0.078125 to 0.078125
- w_rate: bfloat16 [5120, 48], replicated, may hold values from -0.078125 to 0.078125
- rate_bias: float32 [48], P('tensor'), may hold values from -4 to 1
- fast_gate: float32 [16, 320, 320], P('tensor'), may hold values from -0.3125 to 0.3125
- fast_lift: float32 [16, 320, 320], P('tensor'), may hold values from -0.3125 to 0.3125
- fast_down: float32 [16, 320, 320], P('tensor'), may hold values from -0.3125 to 0.3125
- out_gain: float32 [5120], P('tensor'), may hold values from 0.5 to 1.5
Outputs:
- outputs: bfloat16 [2, 1536, 5120], P(None, 'tokens', 'tensor')
The draws below stay inside these ranges and needn't reach their ends.
Inputs may be any that keep to these rules, and one draw needn't show every extreme that they name: E4M3 codes: bit 7 is the sign, bits 3 to 6 the exponent, bits 0 to 2 the mantissa; 127 and 255 never occur.
All inputs are finite; a program needn't handle non-finite values.
Results may differ from the reference program's by a relative error of at most 0.039.
Values may be sent and summed in bfloat16 or wider, within the bound.
No kernel may reach another device: no remote copies, remote signals or barrier semaphores. Data moves between devices by JAX's collectives and lax.ppermute only.
A program may use at most 128 MiB of HBM per device.

```python
import math
import jax
import jax.numpy as jnp
from jax import lax

H = 16
HD = 320
FH = 320
D = 5120
SPANS = 2
SPAN = 1536


def draw_codes(key, part):
    magnitude_key = jax.random.fold_in(key, 11)
    sign_key = jax.random.fold_in(key, 23)
    magnitude = jax.random.randint(magnitude_key, (SPANS, SPAN, D), 0, 127)
    negative = jax.random.randint(sign_key, (SPANS, SPAN, D), 0, 2)
    return (magnitude + 128 * negative).astype(jnp.int32)


def plant(entries, key, low, high):
    extent = entries.shape
    place = [jax.random.randint(jax.random.fold_in(key, axis), (), 0, extent[axis]) for axis in range(len(extent))]
    entries = entries.at[tuple(place)].set(low)
    longest = extent.index(max(extent))
    place[longest] = (place[longest] + 1) % extent[longest]
    return entries.at[tuple(place)].set(high)


def level_of(key, dims, shards, smallest, largest):
    def one(position, shards_of):
        draws = jax.random.uniform(jax.random.fold_in(jax.random.fold_in(key, 6), position), (shards_of,), jnp.float32, smallest / len(shards), largest / len(shards))
        return jnp.repeat(jnp.exp(draws), dims[position] // shards_of).reshape((-1,) + (1,) * (len(dims) - position - 1))

    level = one(*shards[0])
    for cut in shards[1:]:
        level = level * one(*cut)
    return level


def normal_values(stream_key, shape, deviation, most, split=(), kind=jnp.bfloat16):
    loudness = level_of(stream_key, shape, split, -0.22, 0.18) if split else 1.0
    result = jax.random.normal(stream_key, shape, jnp.float32) * deviation * loudness
    return jnp.minimum(jnp.maximum(result, -most), most).astype(kind)


def setup_inputs(seed: int = 0) -> dict:
    seeds = jax.random.split(jax.random.key(seed), 10)
    return {
        "codes": draw_codes(jax.random.fold_in(seeds[9], 71), 0),
        "scales": plant(jax.random.randint(seeds[1], (SPANS, SPAN, D // 32), 119, 123), jax.random.fold_in(seeds[1], 1), 119, 122).astype(jnp.int32),
        "w_qkv": normal_values(seeds[2], (D, 3 * D), D ** -0.5, 0.078125, ((1, 8),)),
        "w_rate": normal_values(seeds[3], (D, 3 * H), D ** -0.5, 0.078125),
        "rate_bias": jnp.clip(-4.0 + 5.0 * jax.random.uniform(seeds[4], (3 * H,), jnp.float32) ** level_of(seeds[4], (3 * H,), ((0, 8),), -0.2, 0.2), -4.0, 1.0),
        "fast_gate": normal_values(seeds[5], (H, HD, FH), HD ** -0.5, 0.3125, ((0, 8),), jnp.float32),
        "fast_lift": normal_values(seeds[6], (H, HD, FH), HD ** -0.5, 0.3125, ((0, 8),), jnp.float32),
        "fast_down": normal_values(seeds[7], (H, FH, HD), FH ** -0.5, 0.3125, ((0, 8),), jnp.float32),
        "out_gain": jnp.clip(1.0 + 0.1 * jax.random.normal(seeds[8], (D,), jnp.float32), 0.5, 1.5),
    }


epsilon = 1e-06
rate_base = 0.15

def dequantize(codes, scales):
    negative = jnp.where(codes >= 128, -1, 1).astype(jnp.int32)
    lower = codes % 128
    exponent = lower // 8
    mantissa = lower % 8
    significand = jnp.where(exponent == 0, mantissa, mantissa + 8) * negative
    shift_part = jnp.maximum(exponent, 1) - 1
    shape = codes.shape
    grouped = significand.reshape(shape[:-1] + (shape[-1] // 32, 32))
    shifts = shift_part.reshape(shape[:-1] + (shape[-1] // 32, 32)) + (scales - 119)[..., None]
    whole = grouped * jnp.left_shift(jnp.ones_like(shifts), shifts)
    values = whole.astype(jnp.float32) * (1.0 / 131072.0)
    return values.reshape(shape).astype(jnp.bfloat16)

def rms_norm(field):
    return field * lax.rsqrt(lax.optimization_barrier(jnp.mean(field * field, axis=-1, keepdims=True)) + epsilon)

def renorm(old, delta):
    summed = old + delta
    old_scale = jnp.sqrt(lax.optimization_barrier(jnp.mean(old * old, axis=-1, keepdims=True)) + epsilon)
    return summed * old_scale * lax.rsqrt(lax.optimization_barrier(jnp.mean(summed * summed, axis=-1, keepdims=True)) + epsilon)

def reference(codes, scales, w_qkv, w_rate, rate_bias, fast_gate, fast_lift, fast_down, out_gain):
    activations = dequantize(codes, scales)
    rate_logits = jnp.dot(activations, w_rate, preferred_element_type=jnp.float32)
    factor = rate_base / math.sqrt(SPAN)

    def head_pass(head_idx):
        columns = lax.dynamic_slice_in_dim(w_qkv, head_idx * (3 * HD), 3 * HD, 1)
        logits = lax.dynamic_slice_in_dim(rate_logits, head_idx * 3, 3, 2)
        bias = lax.dynamic_slice_in_dim(rate_bias, head_idx * 3, 3, 0)
        gain = lax.dynamic_slice_in_dim(out_gain, head_idx * HD, HD, 0)
        gate_w = fast_gate[head_idx]
        lift_w = fast_lift[head_idx]
        down_w = fast_down[head_idx]
        results = []
        for block in range(SPANS):
            projected = jnp.dot(activations[block], columns, preferred_element_type=jnp.float32).astype(jnp.bfloat16)
            queries = projected[:, :HD]
            key_rows = projected[:, HD:2 * HD]
            value_rows = projected[:, 2 * HD:]
            query_norm = rms_norm(queries.astype(jnp.float32)).astype(jnp.bfloat16)
            key_norm = rms_norm(key_rows.astype(jnp.float32)).astype(jnp.bfloat16)
            rates_now = jax.nn.softplus(logits[block] + bias) * factor
            gate_b = gate_w.astype(jnp.bfloat16)
            lift_b = lift_w.astype(jnp.bfloat16)
            down_b = down_w.astype(jnp.bfloat16)
            gate_pre = jnp.dot(key_norm, gate_b, preferred_element_type=jnp.float32)
            lift_pre = jnp.dot(key_norm, lift_b, preferred_element_type=jnp.float32)
            gate_sig = jax.nn.sigmoid(gate_pre)
            activated = gate_pre * gate_sig
            hidden = (activated * lift_pre).astype(jnp.bfloat16)
            hidden_grad = jnp.dot(value_rows, down_b.T, preferred_element_type=jnp.float32)
            gate_grad = (hidden_grad * lift_pre * gate_sig * (1.0 + gate_pre * (1.0 - gate_sig))).astype(jnp.bfloat16)
            lift_grad = (hidden_grad * activated).astype(jnp.bfloat16)
            key_gate = (key_norm.astype(jnp.float32) * rates_now[:, 0:1]).astype(jnp.bfloat16)
            key_lift = (key_norm.astype(jnp.float32) * rates_now[:, 1:2]).astype(jnp.bfloat16)
            hidden_rate = (hidden.astype(jnp.float32) * rates_now[:, 2:3]).astype(jnp.bfloat16)
            delta_gate = jnp.dot(key_gate.T, gate_grad, preferred_element_type=jnp.float32)
            delta_lift = jnp.dot(key_lift.T, lift_grad, preferred_element_type=jnp.float32)
            delta_down = jnp.dot(hidden_rate.T, value_rows, preferred_element_type=jnp.float32)
            gate_w = renorm(gate_w, delta_gate)
            lift_w = renorm(lift_w, delta_lift)
            down_w = renorm(down_w, delta_down)
            query_gate = jnp.dot(query_norm, gate_w.astype(jnp.bfloat16), preferred_element_type=jnp.float32)
            query_lift = jnp.dot(query_norm, lift_w.astype(jnp.bfloat16), preferred_element_type=jnp.float32)
            query_hidden = (jax.nn.silu(query_gate) * query_lift).astype(jnp.bfloat16)
            fast_out = jnp.dot(query_hidden, down_w.astype(jnp.bfloat16), preferred_element_type=jnp.float32)
            results.append((rms_norm(fast_out) * gain).astype(jnp.bfloat16))
        return jnp.stack(results, 0)
    per_head = lax.map(head_pass, jnp.arange(H, dtype=jnp.int32))
    return jnp.transpose(per_head, (1, 2, 0, 3)).reshape(SPANS, SPAN, D)
```

```python
import functools
import math

import jax
import jax.numpy as jnp
from jax import lax
from jax.experimental import pallas as pl
from jax.experimental.pallas import tpu as pltpu
from jax.sharding import PartitionSpec as P

epsilon = 1e-06
rate_base = 0.15
F32 = jnp.float32
BF16 = jnp.bfloat16
MB = 1 << 20


def params(limit):
    return pltpu.CompilerParams(vmem_limit_bytes=limit * MB)


def cost(flops, nbytes):
    return pl.CostEstimate(flops=int(flops), bytes_accessed=int(nbytes), transcendentals=0)


def decode_body(codes_ref, scales_ref, out_ref):
    cols = out_ref.shape[1]
    groups = scales_ref.shape[1]
    first = pl.program_id(0) * (cols // 32)
    lane = lax.broadcasted_iota(jnp.int32, (groups, cols), 1) // 32 + first
    row = lax.broadcasted_iota(jnp.int32, (groups, cols), 0)
    spread = jnp.where(lane == row, 1.0, 0.0).astype(BF16)
    scales = scales_ref[...]
    power = jnp.left_shift(jnp.ones_like(scales), scales - 119).astype(F32).astype(BF16)
    factor = jnp.dot(power, spread, preferred_element_type=F32) * (1.0 / 131072.0)
    codes = codes_ref[...]
    lower = codes & 127
    exponent = lower >> 3
    mantissa = lower & 7
    significand = jnp.where(exponent == 0, mantissa, mantissa + 8)
    whole = jnp.left_shift(significand, jnp.maximum(exponent, 1) - 1)
    signed = jnp.where(codes >= 128, -whole, whole)
    out_ref[...] = (signed.astype(F32) * factor).astype(BF16)


def decode(codes, scales, block):
    rows, width = codes.shape[1:]
    groups = scales.shape[2]
    steps = 4
    cols = width // steps
    return pl.pallas_call(
        decode_body,
        out_shape=jax.ShapeDtypeStruct((rows, width), BF16),
        grid=(steps,),
        in_specs=[
            pl.BlockSpec((None, rows, cols), lambda i: (block, 0, i)),
            pl.BlockSpec((None, rows, groups), lambda i: (block, 0, 0)),
        ],
        out_specs=pl.BlockSpec((rows, cols), lambda i: (0, i)),
        compiler_params=params(16),
        cost_estimate=cost(2e7, rows * width * 6),
        name="decode",
    )(codes, scales)


def rms(field):
    return field * lax.rsqrt(jnp.mean(field * field, axis=-1, keepdims=True) + epsilon)


def project_body(count, heads, size, factor, *refs):
    pieces = refs[:count]
    w_ref, w_rate_ref, bias_ref, q_ref, k_ref, v_ref, rate_ref, acc_ref, logit_ref = refs[count:]
    step = pl.program_id(0)
    rows = jnp.concatenate([piece[...] for piece in pieces], axis=0)
    part = jnp.dot(rows, w_ref[...], preferred_element_type=F32)
    logit = jnp.dot(rows, w_rate_ref[...], preferred_element_type=F32)

    @pl.when(step == 0)
    def _():
        acc_ref[...] = part
        logit_ref[...] = logit

    @pl.when(step > 0)
    def _():
        acc_ref[...] += part
        logit_ref[...] += logit

    @pl.when(step == pl.num_programs(0) - 1)
    def _():
        for head in range(heads):
            base = 3 * size * head
            query = acc_ref[:, base : base + size].astype(BF16).astype(F32)
            key = acc_ref[:, base + size : base + 2 * size].astype(BF16).astype(F32)
            q_ref[head] = rms(query).astype(BF16)
            k_ref[head] = rms(key).astype(BF16)
            v_ref[head] = acc_ref[:, base + 2 * size : base + 3 * size].astype(BF16)
        rate_ref[...] = jax.nn.softplus(logit_ref[...] + bias_ref[...]) * factor


def project(pieces, w, w_rate, bias, heads, size, factor):
    rows, width = pieces[0].shape
    total = rows * len(pieces)
    steps = 8
    depth = width // steps
    columns = w.shape[1]
    lanes = w_rate.shape[1]
    return pl.pallas_call(
        functools.partial(project_body, len(pieces), heads, size, factor),
        out_shape=[jax.ShapeDtypeStruct((heads, total, size), BF16)] * 3
        + [jax.ShapeDtypeStruct((total, lanes), F32)],
        grid=(steps,),
        in_specs=[pl.BlockSpec((rows, depth), lambda i: (0, i))] * len(pieces)
        + [
            pl.BlockSpec((depth, columns), lambda i: (i, 0)),
            pl.BlockSpec((depth, lanes), lambda i: (i, 0)),
            pl.BlockSpec((1, lanes), lambda i: (0, 0)),
        ],
        out_specs=[pl.BlockSpec((heads, total, size), lambda i: (0, 0, 0))] * 3
        + [pl.BlockSpec((total, lanes), lambda i: (0, 0))],
        scratch_shapes=[pltpu.VMEM((total, columns), F32), pltpu.VMEM((total, lanes), F32)],
        compiler_params=params(28),
        cost_estimate=cost(2 * total * width * columns, width * columns * 2),
        name="project",
    )(*pieces, w, w_rate, bias)


def stack_rows(refs, full_ref, me, n, part):
    for k in range(n):
        at = pl.multiple_of((me ^ k) * part, part)
        full_ref[pl.ds(at, part), :] = refs[k][...]


def update_body(n, heads, size, chunks, fresh, *refs):
    me_ref = refs[0]
    refs = refs[1:]
    me = me_ref[0]
    kvr = refs[: 3 * chunks]
    refs = refs[3 * chunks :]
    many = 3 if fresh else n
    weights = refs[:many]
    refs = refs[many:]
    outs = refs[:n]
    full_ref, delta_ref = refs[n:]
    part = full_ref.shape[0] // n
    mats = heads * size
    if fresh:
        for i in range(3):
            full_ref[i * mats : (i + 1) * mats, :] = weights[i][...].astype(BF16)
    else:
        stack_rows(weights, full_ref, me, n, part)
    for head in range(heads):
        first = head * size
        gate = full_ref[first : first + size, :]
        lift = full_ref[mats + first : mats + first + size, :]
        down = full_ref[2 * mats + first : 2 * mats + first + size, :]
        sums = [None, None, None]
        for c in range(chunks):
            k_ref, v_ref, rate_ref = kvr[3 * c : 3 * c + 3]
            key = k_ref[head]
            value = v_ref[head]
            key32 = key.astype(F32)
            rate = rate_ref[:, 3 * head : 3 * head + 3]
            gate_pre = jnp.dot(key, gate, preferred_element_type=F32)
            lift_pre = jnp.dot(key, lift, preferred_element_type=F32)
            hidden_grad = lax.dot_general(
                value, down, (((1,), (1,)), ((), ())), preferred_element_type=F32
            )
            sig = jax.nn.sigmoid(gate_pre)
            activated = gate_pre * sig
            hidden = (activated * lift_pre).astype(BF16)
            gate_grad = (hidden_grad * lift_pre * sig * (1.0 + gate_pre * (1.0 - sig))).astype(BF16)
            lift_grad = (hidden_grad * activated).astype(BF16)
            key_gate = (key32 * rate[:, 0:1]).astype(BF16)
            key_lift = (key32 * rate[:, 1:2]).astype(BF16)
            hidden_rate = (hidden.astype(F32) * rate[:, 2:3]).astype(BF16)
            pairs = ((key_gate, gate_grad), (key_lift, lift_grad), (hidden_rate, value))
            for i, (left, right) in enumerate(pairs):
                term = lax.dot_general(
                    left, right, (((0,), (0,)), ((), ())), preferred_element_type=F32
                )
                sums[i] = term if sums[i] is None else sums[i] + term
        for i in range(3):
            delta_ref[i * mats + first : i * mats + first + size, :] = sums[i]
    for k in range(n):
        at = pl.multiple_of((me ^ k) * part, part)
        outs[k][...] = delta_ref[pl.ds(at, part), :].astype(outs[k].dtype)


def whole(array):
    rank = len(array.shape)
    return pl.BlockSpec(array.shape, lambda *_: (0,) * rank)


def update(me, kvr, weights, n, heads, size, fresh):
    flat = [a for group in kvr for a in group]
    total = 3 * heads * size
    part = total // n
    outs = [jax.ShapeDtypeStruct((part, size), F32)] + [
        jax.ShapeDtypeStruct((part, size), BF16)
    ] * (n - 1)
    args = flat + list(weights)
    tokens = sum(a.shape[0] for a in (g[2] for g in kvr))
    return pl.pallas_call(
        functools.partial(update_body, n, heads, size, len(kvr), fresh),
        out_shape=outs,
        grid_spec=pltpu.PrefetchScalarGridSpec(
            num_scalar_prefetch=1,
            grid=(1,),
            in_specs=[whole(a) for a in args],
            out_specs=[whole(a) for a in outs],
            scratch_shapes=[pltpu.VMEM((total, size), BF16), pltpu.VMEM((total, size), F32)],
        ),
        compiler_params=params(28),
        cost_estimate=cost(4e9 * tokens / 384, 8e6),
        name="update",
    )(me, *args)


def renorm_body(n, *refs):
    own_ref = refs[0]
    got = refs[1:n]
    old_ref, new_ref, round_ref = refs[n:]
    delta = own_ref[...]
    for ref in got:
        delta = delta + ref[...].astype(F32)
    old = old_ref[...]
    summed = old + delta
    old_scale = jnp.sqrt(jnp.mean(old * old, axis=-1, keepdims=True) + epsilon)
    new = summed * old_scale * lax.rsqrt(
        jnp.mean(summed * summed, axis=-1, keepdims=True) + epsilon
    )
    new_ref[...] = new
    round_ref[...] = new.astype(BF16)


def renorm(parts, old):
    args = list(parts) + [old]
    outs = [jax.ShapeDtypeStruct(old.shape, F32), jax.ShapeDtypeStruct(old.shape, BF16)]
    return pl.pallas_call(
        functools.partial(renorm_body, len(parts)),
        out_shape=outs,
        grid=(1,),
        in_specs=[whole(a) for a in args],
        out_specs=[whole(a) for a in outs],
        compiler_params=params(16),
        cost_estimate=cost(2e6, 4e6),
        name="renorm",
    )(*args)


def answer_body(n, heads, size, chunks, places, chained, *refs):
    at_ref = refs[0]
    refs = refs[1:]
    queries = refs[:chunks]
    weights = refs[chunks : chunks + n]
    gain_ref = refs[chunks + n]
    refs = refs[chunks + n + (2 if chained else 1) :]
    out_ref, full_ref = refs
    part = full_ref.shape[0] // n
    me = at_ref[0]
    mats = heads * size
    stack_rows(weights, full_ref, me, n, part)
    piece = out_ref.shape[0] // places
    place = 0
    for c in range(chunks):
        count = queries[c].shape[1] // piece
        normed = []
        for head in range(heads):
            first = head * size
            query = queries[c][head]
            gate = full_ref[first : first + size, :]
            lift = full_ref[mats + first : mats + first + size, :]
            down = full_ref[2 * mats + first : 2 * mats + first + size, :]
            query_gate = jnp.dot(query, gate, preferred_element_type=F32)
            query_lift = jnp.dot(query, lift, preferred_element_type=F32)
            hidden = (query_gate * jax.nn.sigmoid(query_gate) * query_lift).astype(BF16)
            fast = jnp.dot(hidden, down, preferred_element_type=F32)
            normed.append((rms(fast) * gain_ref[head : head + 1, :]).astype(BF16))
        row = jnp.concatenate(normed, axis=1)
        for i in range(count):
            at = pl.multiple_of(at_ref[1 + place] * piece, piece)
            out_ref[pl.ds(at, piece), :] = row[i * piece : (i + 1) * piece, :]
            place += 1


def answer(at, queries, weights, gain, n, heads, size, places, block, blocks, before):
    tokens = sum(q.shape[1] for q in queries)
    args = list(queries) + list(weights) + [gain]
    specs = [whole(a) for a in args]
    chained = before is not None
    alias = {}
    if chained:
        specs.append(pl.BlockSpec(memory_space=pl.ANY))
        alias = {1 + len(args): 0}
        args.append(before)
    return pl.pallas_call(
        functools.partial(answer_body, n, heads, size, len(queries), places, chained),
        out_shape=jax.ShapeDtypeStruct((blocks, tokens, heads * size), BF16),
        grid_spec=pltpu.PrefetchScalarGridSpec(
            num_scalar_prefetch=1,
            grid=(1,),
            in_specs=specs,
            out_specs=pl.BlockSpec((None, tokens, heads * size), lambda *_: (block, 0, 0)),
            scratch_shapes=[pltpu.VMEM((3 * heads * size, size), BF16)],
        ),
        input_output_aliases=alias,
        compiler_params=params(28),
        cost_estimate=cost(2e9 * tokens / 384, 4e6),
        name="answer",
    )(at, *args)


def chips(pairs):
    return [(2 * a + c, 2 * b + c) for a, b in pairs for c in (0, 1)]


def line_gather(rows, side):
    first = lax.ppermute(rows, "tensor", chips([(1, 0), (3, 1), (0, 2), (2, 3)]))
    ends = lax.ppermute(first, "tensor", chips([(1, 0), (2, 3)]))
    mids = lax.ppermute(rows, "tensor", chips([(1, 2), (2, 1)]))
    last = lax.ppermute(rows, "tensor", chips([(2, 0), (0, 1), (3, 2), (1, 3)]))
    second = ends + mids
    return [rows, first, second, last]


def gather(rows):
    n = lax.axis_size("tensor")
    side = [(t, t ^ 1) for t in range(n)]
    outer = n // 2
    if outer == 4:
        got = line_gather(rows, side)
    else:
        got = [rows] + [
            lax.ppermute(rows, "tensor", chips([(z, (z + k) % outer) for z in range(outer)]))
            for k in range(1, outer)
        ]
    pieces = []
    for piece in got:
        pieces += [piece, lax.ppermute(piece, "tensor", side)]
    return pieces


def sources():
    n = lax.axis_size("tensor")
    mine = lax.axis_index("tensor")
    outer = n // 2
    chip, core = mine // 2, mine % 2
    if outer == 4:
        tables = ((0, 1, 2, 3), (1, 3, 0, 2), (3, 2, 1, 0), (2, 0, 3, 1))
        chip_of = [jnp.asarray(t, jnp.int32)[chip] for t in tables]
    else:
        chip_of = [(chip - k) % outer for k in range(outer)]
    found = []
    for c in chip_of:
        found += [c * 2 + core, c * 2 + (1 - core)]
    return jnp.stack([x.astype(jnp.int32) for x in found])


def swap(array, k):
    n = lax.axis_size("tokens")
    return lax.ppermute(array, "tokens", [(t, t ^ k) for t in range(n)])


def local(codes, scales, w_qkv, w_rate, rate_bias, fast_gate, fast_lift, fast_down, out_gain):
    blocks = codes.shape[0]
    heads, size = fast_gate.shape[:2]
    n = lax.axis_size("tokens")
    tokens = codes.shape[1] * lax.axis_size("tensor")
    factor = rate_base / math.sqrt(tokens * n)
    token = lax.axis_index("tokens").astype(jnp.int32)
    lanes = 3 * heads
    rate_cols = lax.dynamic_slice_in_dim(w_rate, lax.axis_index("tensor") * lanes, lanes, 1)
    bias = rate_bias.reshape(1, lanes)
    gain = out_gain.reshape(heads, size)
    flat = [m.reshape(heads * size, m.shape[-1]) for m in (fast_gate, fast_lift, fast_down)]
    part = 3 * heads * size // n
    state = lax.dynamic_slice_in_dim(jnp.concatenate(flat, 0), token * part, part, 0)
    me = token.reshape(1)
    at = jnp.concatenate([me, sources()])

    out = None
    weights = flat
    for block in range(blocks):
        pieces = gather(decode(codes, scales, block))
        half = len(pieces) // 2
        chunks = [
            project(group, w_qkv, rate_cols, bias, heads, size, factor)
            for group in (pieces[:half], pieces[half:])
        ]
        deltas = update(me, [c[1:4] for c in chunks], weights, n, heads, size, block == 0)
        parts = [deltas[0]] + [swap(deltas[k], k) for k in range(1, n)]
        state, rounded = renorm(parts, state)
        weights = [rounded] + [swap(rounded, k) for k in range(1, n)]
        out = answer(
            at, [c[0] for c in chunks], weights, gain, n, heads, size, len(pieces), block, blocks, out
        )
    return out


def solution(mesh):
    return jax.shard_map(
        local,
        mesh=mesh,
        in_specs=(
            P(None, ("tokens", "tensor"), None),
            P(None, ("tokens", "tensor"), None),
            P(None, "tensor"),
            P(),
            P("tensor"),
            P("tensor", None, None),
            P("tensor", None, None),
            P("tensor", None, None),
            P("tensor"),
        ),
        out_specs=P(None, "tokens", "tensor"),
        check_vma=False,
    )
```

```python
import functools
import math

import jax
import jax.numpy as jnp
from jax import lax
from jax.experimental import pallas as pl
from jax.experimental.pallas import tpu as pltpu
from jax.sharding import PartitionSpec as P


epsilon = 1e-06
rate_base = 0.15
F32 = jnp.float32
BF16 = jnp.bfloat16
MB = 1 << 20


VMEM = pl.BlockSpec(memory_space=pltpu.VMEM)


def params(limit):
    return pltpu.CompilerParams(vmem_limit_bytes=limit * MB)


def cost(flops, nbytes):
    return pl.CostEstimate(flops=int(flops), bytes_accessed=int(nbytes), transcendentals=0)


def decode_body(codes_ref, scales_ref, out_ref):
    cols = out_ref.shape[1]
    groups = scales_ref.shape[1]
    first = pl.program_id(0) * (cols // 32)
    lane = lax.broadcasted_iota(jnp.int32, (groups, cols), 1) // 32 + first
    row = lax.broadcasted_iota(jnp.int32, (groups, cols), 0)
    spread = jnp.where(lane == row, 1.0, 0.0).astype(BF16)
    scales = scales_ref[...]
    power = jnp.left_shift(jnp.ones_like(scales), scales - 119).astype(F32).astype(BF16)
    factor = jnp.dot(power, spread, preferred_element_type=F32) * (1.0 / 131072.0)
    codes = codes_ref[...]
    lower = codes & 127
    exponent = lower >> 3
    mantissa = lower & 7
    significand = jnp.where(exponent == 0, mantissa, mantissa + 8)
    whole = jnp.left_shift(significand, jnp.maximum(exponent, 1) - 1)
    signed = jnp.where(codes >= 128, -whole, whole)
    out_ref[...] = (signed.astype(F32) * factor).astype(BF16)


def decode(codes, scales, block):
    codes = pltpu.with_memory_space_constraint(codes, pltpu.HBM)
    scales = pltpu.with_memory_space_constraint(scales, pltpu.HBM)
    rows, width = codes.shape[1:]
    groups = scales.shape[2]
    steps = 4
    cols = width // steps
    return pl.pallas_call(
        decode_body,
        out_shape=jax.ShapeDtypeStruct((rows, width), BF16),
        grid=(steps,),
        in_specs=[
            pl.BlockSpec((None, rows, cols), lambda i: (block, 0, i)),
            pl.BlockSpec((None, rows, groups), lambda i: (block, 0, 0)),
        ],
        out_specs=pl.BlockSpec((rows, cols), lambda i: (0, i)),
        compiler_params=params(4),
        cost_estimate=cost(2e7, rows * width * 6),
        name="decode",
    )(codes, scales)


def pick_body(rows_ref, out_ref):
    count = out_ref.shape[0]
    first = lax.axis_index("tensor") * (rows_ref.shape[0] // lax.axis_size("tensor"))
    row = lax.broadcasted_iota(jnp.int32, (count, rows_ref.shape[0]), 0) + first
    column = lax.broadcasted_iota(jnp.int32, (count, rows_ref.shape[0]), 1)
    hot = jnp.where(row == column, 1.0, 0.0).astype(BF16)
    out_ref[...] = jnp.dot(hot, rows_ref[...], preferred_element_type=F32).astype(BF16)


def pick(w_rate, lanes):
    count = -(-lanes // 16) * 16
    return pl.pallas_call(
        pick_body,
        out_shape=jax.ShapeDtypeStruct((count, w_rate.shape[0]), BF16),
        in_specs=[VMEM],
        out_specs=VMEM,
        compiler_params=params(4),
        name="pick",
    )(w_rate.T)


def load_body(from_ref, out_ref, sem):
    copy = pltpu.make_async_copy(from_ref, out_ref, sem)
    copy.start()
    copy.wait()


def load(array):
    return pl.pallas_call(
        load_body,
        out_shape=jax.ShapeDtypeStruct(array.shape, array.dtype),
        in_specs=[pl.BlockSpec(memory_space=pl.ANY)],
        out_specs=VMEM,
        scratch_shapes=[pltpu.SemaphoreType.DMA],
        compiler_params=params(6),
        cost_estimate=cost(0, 2 * array.size),
        name="load",
    )(pltpu.with_memory_space_constraint(array, pltpu.HBM))


def add_body(left_ref, right_ref, out_ref):
    out_ref[...] = left_ref[...] + right_ref[...]


def add(left, right):
    return pl.pallas_call(
        add_body,
        out_shape=jax.ShapeDtypeStruct(left.shape, left.dtype),
        in_specs=[VMEM] * 2,
        out_specs=VMEM,
        compiler_params=params(4),
        name="add",
    )(left, right)


def rms(field):
    return field * lax.rsqrt(jnp.mean(field * field, axis=-1, keepdims=True) + epsilon)


def project_body(count, heads, size, factor, *refs):
    pieces = refs[:count]
    w_ref, w_rate_ref, bias_ref, q_ref, k_ref, v_ref, rate_ref = refs[count:]
    rows = jnp.concatenate([piece[...] for piece in pieces], axis=0)
    logits = lax.dot_general(
        rows, w_rate_ref[...], (((1,), (1,)), ((), ())), preferred_element_type=F32
    )
    lanes = rate_ref.shape[1]
    rate_ref[...] = jax.nn.softplus(logits[:, :lanes] + bias_ref[...].reshape(1, lanes)) * factor
    projected = jnp.dot(rows, w_ref[...], preferred_element_type=F32)
    for head in range(heads):
        base = 3 * size * head
        query = projected[:, base : base + size].astype(BF16).astype(F32)
        key = projected[:, base + size : base + 2 * size].astype(BF16).astype(F32)
        q_ref[head] = rms(query).astype(BF16)
        k_ref[head] = rms(key).astype(BF16)
        v_ref[head] = projected[:, base + 2 * size : base + 3 * size].astype(BF16)


def project(pieces, w, w_rate, bias, heads, size, factor):
    rows, width = pieces[0].shape
    total = rows * len(pieces)
    columns = w.shape[1]
    lanes = 3 * heads
    return pl.pallas_call(
        functools.partial(project_body, len(pieces), heads, size, factor),
        out_shape=[jax.ShapeDtypeStruct((heads, total, size), BF16)] * 3
        + [jax.ShapeDtypeStruct((total, lanes), F32)],
        in_specs=[VMEM] * (len(pieces) + 3),
        out_specs=[VMEM] * 4,
        compiler_params=params(-(-6 * total * width // MB)),
        cost_estimate=cost(2 * total * width * columns, width * columns * 2),
        name="project",
    )(*pieces, w, w_rate, bias)


def stack_rows(refs, full_ref, me, part):
    for k, ref in enumerate(refs):
        at = pl.multiple_of((me ^ k) * part, part)
        full_ref[pl.ds(at, part), :] = ref[...]


def update_body(n, head, size, chunks, fresh, *refs):
    me = lax.axis_index("tokens").astype(jnp.int32)
    kvr = refs[: 3 * chunks]
    refs = refs[3 * chunks :]
    many = 3 if fresh else n
    weights = refs[:many]
    refs = refs[many:]
    outs = refs[:n]
    full_ref, delta_ref = refs[-2:]
    part = full_ref.shape[0] // n
    if fresh:
        for i in range(3):
            matrix = weights[i][head]
            full_ref[i * size : (i + 1) * size, :] = matrix.astype(BF16)
            delta_ref[i * size : (i + 1) * size, :] = matrix
        refs[n][...] = delta_ref[pl.ds(pl.multiple_of(me * part, part), part), :]
    else:
        stack_rows(weights, full_ref, me, part)
    gate = full_ref[:size, :]
    lift = full_ref[size : 2 * size, :]
    down = full_ref[2 * size :, :]
    sums = [None, None, None]
    for c in range(chunks):
        k_ref, v_ref, rate_ref = kvr[3 * c : 3 * c + 3]
        key = k_ref[head]
        value = v_ref[head]
        key32 = key.astype(F32)
        rate = rate_ref[:, 3 * head : 3 * head + 3]
        gate_pre = jnp.dot(key, gate, preferred_element_type=F32)
        lift_pre = jnp.dot(key, lift, preferred_element_type=F32)
        hidden_grad = lax.dot_general(
            value, down, (((1,), (1,)), ((), ())), preferred_element_type=F32
        )
        sig = jax.nn.sigmoid(gate_pre)
        activated = gate_pre * sig
        hidden = (activated * lift_pre).astype(BF16)
        gate_grad = (hidden_grad * lift_pre * sig * (1.0 + gate_pre * (1.0 - sig))).astype(BF16)
        lift_grad = (hidden_grad * activated).astype(BF16)
        key_gate = (key32 * rate[:, 0:1]).astype(BF16)
        key_lift = (key32 * rate[:, 1:2]).astype(BF16)
        hidden_rate = (hidden.astype(F32) * rate[:, 2:3]).astype(BF16)
        pairs = ((key_gate, gate_grad), (key_lift, lift_grad), (hidden_rate, value))
        for i, (left, right) in enumerate(pairs):
            term = lax.dot_general(
                left, right, (((0,), (0,)), ((), ())), preferred_element_type=F32
            )
            sums[i] = term if sums[i] is None else sums[i] + term
    for i in range(3):
        delta_ref[i * size : (i + 1) * size, :] = sums[i]
    for k in range(n):
        at = pl.multiple_of((me ^ k) * part, part)
        outs[k][...] = delta_ref[pl.ds(at, part), :].astype(outs[k].dtype)


def update(kvr, weights, n, head, size, fresh):
    flat = [a for group in kvr for a in group]
    total = 3 * size
    part = total // n
    outs = [jax.ShapeDtypeStruct((part, size), F32)] + [
        jax.ShapeDtypeStruct((part, size), BF16)
    ] * (n - 1)
    if fresh:
        outs.append(outs[0])
    args = flat + list(weights)
    tokens = sum(g[2].shape[0] for g in kvr)
    return pl.pallas_call(
        functools.partial(update_body, n, head, size, len(kvr), fresh),
        out_shape=outs,
        in_specs=[VMEM] * len(args),
        out_specs=[VMEM] * len(outs),
        scratch_shapes=[pltpu.VMEM((total, size), BF16), pltpu.VMEM((total, size), F32)],
        compiler_params=params(-(-48 * tokens * size // MB)),
        cost_estimate=cost(2e9 * tokens / 384, 4e6),
        name="update",
    )(*args)


def renorm_body(n, *refs):
    old_ref, new_ref, round_ref = refs[n:]
    delta = refs[0][...]
    for ref in refs[1:n]:
        delta = delta + ref[...].astype(F32)
    old = old_ref[...]
    summed = old + delta
    old_scale = jnp.sqrt(jnp.mean(old * old, axis=-1, keepdims=True) + epsilon)
    new = summed * old_scale * lax.rsqrt(
        jnp.mean(summed * summed, axis=-1, keepdims=True) + epsilon
    )
    new_ref[...] = new
    round_ref[...] = new.astype(BF16)


def renorm(parts, old):
    args = list(parts) + [old]
    outs = [jax.ShapeDtypeStruct(old.shape, F32), jax.ShapeDtypeStruct(old.shape, BF16)]
    return pl.pallas_call(
        functools.partial(renorm_body, len(parts)),
        out_shape=outs,
        in_specs=[VMEM] * len(args),
        out_specs=[VMEM] * 2,
        compiler_params=params(4),
        cost_estimate=cost(1e6, 2e6),
        name="renorm",
    )(*args)


def head_gain(gain_ref, head, size):
    return gain_ref[...].reshape(1, -1)[:, head * size : (head + 1) * size]


def fast_rows(query, full_ref, size, gain):
    gate = full_ref[:size, :]
    lift = full_ref[size : 2 * size, :]
    down = full_ref[2 * size :, :]
    query_gate = jnp.dot(query, gate, preferred_element_type=F32)
    query_lift = jnp.dot(query, lift, preferred_element_type=F32)
    hidden = (query_gate * jax.nn.sigmoid(query_gate) * query_lift).astype(BF16)
    fast = jnp.dot(hidden, down, preferred_element_type=F32)
    return (rms(fast) * gain).astype(BF16)


def answer_body(n, head, chunks, *refs):
    me = lax.axis_index("tokens").astype(jnp.int32)
    queries = refs[:chunks]
    weights = refs[chunks : chunks + n]
    gain_ref, out_ref, full_ref = refs[chunks + n :]
    size = full_ref.shape[1]
    stack_rows(weights, full_ref, me, full_ref.shape[0] // n)
    first = 0
    for query_ref in queries:
        rows = query_ref.shape[1]
        normed = fast_rows(query_ref[head], full_ref, size, head_gain(gain_ref, head, size))
        out_ref[first : first + rows, :] = normed
        first += rows


def answer(queries, weights, gain, n, head, size):
    tokens = sum(q.shape[1] for q in queries)
    args = list(queries) + list(weights) + [gain]
    return pl.pallas_call(
        functools.partial(answer_body, n, head, len(queries)),
        out_shape=jax.ShapeDtypeStruct((tokens, size), BF16),
        in_specs=[VMEM] * len(args),
        out_specs=VMEM,
        scratch_shapes=[pltpu.VMEM((3 * size, size), BF16)],
        compiler_params=params(-(-48 * tokens * size // MB)),
        cost_estimate=cost(1e9 * tokens / 384, 2e6),
        name="answer",
    )(*args)


def finish_body(n, head, chunks, places, block, others, chained, *refs):
    me = lax.axis_index("tokens").astype(jnp.int32)
    origin = sources(block)
    queries = refs[:chunks]
    refs = refs[chunks:]
    weights = refs[:n]
    gain_ref = refs[n]
    before = refs[n + 1 : n + 1 + others]
    refs = refs[n + 1 + others + (1 if chained else 0) :]
    out_ref, full_ref, rows_ref, sem = refs
    size = full_ref.shape[1]
    stack_rows(weights, full_ref, me, full_ref.shape[0] // n)
    piece = rows_ref.shape[0] // places
    place = 0
    for query_ref in queries:
        normed = fast_rows(query_ref[head], full_ref, size, head_gain(gain_ref, head, size))
        first = place * piece
        rows = query_ref.shape[1]
        joined = jnp.concatenate([ref[first : first + rows, :] for ref in before] + [normed], axis=1)
        for i in range(rows // piece):
            at = pl.multiple_of(origin[place] * piece, piece)
            rows_ref[pl.ds(at, piece), :] = joined[i * piece : (i + 1) * piece, :]
            place += 1
    copy = pltpu.make_async_copy(rows_ref, out_ref.at[block], sem)
    copy.start()
    copy.wait()


def finish(queries, weights, gain, n, head, size, others, places, block, blocks, before):
    tokens = sum(q.shape[1] for q in queries)
    width = size * (len(others) + 1)
    args = list(queries) + list(weights) + [gain] + list(others)
    specs = [VMEM] * len(args)
    alias = {}
    if before is not None:
        alias = {len(args): 0}
        args.append(before)
        specs.append(pl.BlockSpec(memory_space=pl.ANY))
    return pl.pallas_call(
        functools.partial(
            finish_body, n, head, len(queries), places, block, len(others), before is not None
        ),
        out_shape=jax.ShapeDtypeStruct((blocks, tokens, width), BF16),
        in_specs=specs,
        out_specs=pl.BlockSpec(memory_space=pl.ANY),
        scratch_shapes=[
            pltpu.VMEM((3 * size, size), BF16),
            pltpu.VMEM((tokens, width), BF16),
            pltpu.SemaphoreType.DMA,
        ],
        input_output_aliases=alias,
        compiler_params=params(-(-48 * tokens * size // MB)),
        cost_estimate=cost(1e9 * tokens / 384, 2e6),
        name="finish",
    )(*args)


def chips(pairs):
    return [(2 * a + c, 2 * b + c) for a, b in pairs for c in (0, 1)]


def shift(array, pairs):
    return lax.ppermute(array, "tensor", pairs)


def gather(rows, block):
    n = lax.axis_size("tensor")
    side = [(t, t ^ 1) for t in range(n)]
    outer = n // 2
    if outer == 4:
        first = shift(rows, chips([(1, 0), (3, 1), (0, 2), (2, 3)]))
        ends = shift(first, chips([(1, 0), (2, 3)]))
        mids = shift(rows, chips([(1, 2), (2, 1)]))
        last = shift(rows, chips([(2, 0), (0, 1), (3, 2), (1, 3)]))
        second = add(ends, mids)
        got = [rows, first, second, last] if block == 0 else [rows, first, last, second]
    else:
        got = [rows] + [
            shift(rows, chips([(z, (z + k) % outer) for z in range(outer)]))
            for k in range(1, outer)
        ]
    pieces = []
    for piece in got:
        pieces += [piece, shift(piece, side)]
    return pieces


def sources(block):
    n = lax.axis_size("tensor")
    mine = lax.axis_index("tensor").astype(jnp.int32)
    outer = n // 2
    chip, core = mine // 2, mine % 2
    if outer == 4:
        high, low = chip // 2, chip % 2
        first = jnp.where(high == 0, 1 + 2 * low, 2 * low)
        last = jnp.where(high == 0, 2 - 2 * low, 3 - 2 * low)
        chip_of = [chip, first] + ([3 - chip, last] if block == 0 else [last, 3 - chip])
    else:
        chip_of = [(chip + outer - k) % outer for k in range(outer)]
    found = []
    for c in chip_of:
        found += [c * 2 + core, c * 2 + (1 - core)]
    return found


def swap(array, k):
    n = lax.axis_size("tokens")
    return lax.ppermute(array, "tokens", [(t, t ^ k) for t in range(n)])


def local(codes, scales, w_qkv, w_rate, rate_bias, fast_gate, fast_lift, fast_down, out_gain):
    blocks = codes.shape[0]
    heads, size = fast_gate.shape[:2]
    n = lax.axis_size("tokens")
    tokens = codes.shape[1] * lax.axis_size("tensor")
    factor = rate_base / math.sqrt(tokens * n)
    rate_rows = pick(w_rate, 3 * heads)
    w_qkv = load(w_qkv)
    fresh = [fast_gate, fast_lift, fast_down]
    state = [None] * heads
    weights = [fresh] * heads

    rows = []
    for block in range(blocks):
        rows.append(decode(codes, scales, block))
    out = None
    for block in range(blocks):
        pieces = gather(rows[block], block)
        chunks = []
        for group in (pieces[:-2], pieces[-2:]):
            chunks.append(project(group, w_qkv, rate_rows, rate_bias, heads, size, factor))
        kvr = [c[1:4] for c in chunks]
        queries = [c[0] for c in chunks]
        done = []
        for head in range(heads):
            deltas = update(kvr, weights[head], n, head, size, block == 0)
            if block == 0:
                state[head] = deltas[n]
            parts = [deltas[0]] + [swap(deltas[k], k) for k in range(1, n)]
            state[head], rounded = renorm(parts, state[head])
            weights[head] = [rounded] + [swap(rounded, k) for k in range(1, n)]
            if head < heads - 1:
                done.append(answer(queries, weights[head], out_gain, n, head, size))
            else:
                out = finish(
                    queries, weights[head], out_gain, n, head, size, done, len(pieces), block,
                    blocks, out,
                )
    return out


def solution(mesh):
    return jax.shard_map(
        local,
        mesh=mesh,
        in_specs=(
            P(None, ("tokens", "tensor"), None),
            P(None, ("tokens", "tensor"), None),
            P(None, "tensor"),
            P(),
            P("tensor"),
            P("tensor", None, None),
            P("tensor", None, None),
            P("tensor", None, None),
            P("tensor"),
        ),
        out_specs=P(None, "tokens", "tensor"),
        check_vma=False,
    )
```

```python
import functools
import math

import jax
import jax.numpy as jnp
from jax import lax
from jax.experimental import pallas as pl
from jax.experimental.pallas import tpu as pltpu
from jax.sharding import PartitionSpec as P


epsilon = 1e-06
rate_base = 0.15
F32 = jnp.float32
BF16 = jnp.bfloat16
MB = 1 << 20


VMEM = pl.BlockSpec(memory_space=pltpu.VMEM)


def params(limit):
    return pltpu.CompilerParams(vmem_limit_bytes=limit * MB)


def cost(flops, nbytes):
    return pl.CostEstimate(flops=int(flops), bytes_accessed=int(nbytes), transcendentals=0)


def decode_body(block, steps, codes_hbm, scales_hbm, out_ref, codes_ref, scales_ref, sem):
    cols = out_ref.shape[1] // steps
    groups = cols // 32
    copies = [
        pltpu.make_async_copy(scales_hbm.at[block], scales_ref, sem.at[steps]),
    ]
    for i in range(steps):
        part = pl.ds(i * cols, cols)
        copies.append(
            pltpu.make_async_copy(codes_hbm.at[block, :, part], codes_ref.at[:, part], sem.at[i])
        )
    for copy in copies:
        copy.start()
    lane = lax.broadcasted_iota(jnp.int32, (groups, cols), 1) // 32
    row = lax.broadcasted_iota(jnp.int32, (groups, cols), 0)
    spread = jnp.where(lane == row, 1.0, 0.0).astype(BF16)
    copies[0].wait()
    scales = scales_ref[...]
    power = jnp.left_shift(jnp.ones_like(scales), scales - 119).astype(F32) * (1.0 / 131072.0)
    power = power.astype(BF16)
    for i in range(steps):
        copies[1 + i].wait()
        factor = jnp.dot(
            power[:, i * groups : (i + 1) * groups], spread, preferred_element_type=F32
        )
        codes = codes_ref[:, i * cols : (i + 1) * cols]
        lower = codes & 127
        exponent = lower >> 3
        mantissa = lower & 7
        significand = jnp.where(exponent == 0, mantissa, mantissa + 8)
        whole = jnp.left_shift(significand, jnp.maximum(exponent, 1) - 1)
        signed = jnp.where(codes >= 128, -whole, whole)
        out_ref[:, i * cols : (i + 1) * cols] = (signed.astype(F32) * factor).astype(BF16)


def decode(codes, scales, block):
    rows, width = codes.shape[1:]
    steps = 4
    hbm = pl.BlockSpec(memory_space=pl.ANY)
    return pl.pallas_call(
        functools.partial(decode_body, block, steps),
        out_shape=jax.ShapeDtypeStruct((rows, width), BF16),
        in_specs=[hbm, hbm],
        out_specs=VMEM,
        scratch_shapes=[
            pltpu.VMEM((rows, width), jnp.int32),
            pltpu.VMEM((rows, scales.shape[2]), jnp.int32),
            pltpu.SemaphoreType.DMA((steps + 1,)),
        ],
        compiler_params=params(4),
        cost_estimate=cost(2e7, rows * width * 6),
        name="decode",
    )(
        pltpu.with_memory_space_constraint(codes, pltpu.HBM),
        pltpu.with_memory_space_constraint(scales, pltpu.HBM),
    )


def pick_body(rows_ref, out_ref):
    count = out_ref.shape[0]
    first = lax.axis_index("tensor") * (rows_ref.shape[0] // lax.axis_size("tensor"))
    row = lax.broadcasted_iota(jnp.int32, (count, rows_ref.shape[0]), 0) + first
    column = lax.broadcasted_iota(jnp.int32, (count, rows_ref.shape[0]), 1)
    hot = jnp.where(row == column, 1.0, 0.0).astype(BF16)
    out_ref[...] = jnp.dot(hot, rows_ref[...], preferred_element_type=F32).astype(BF16)


def pick(w_rate, lanes):
    count = -(-lanes // 16) * 16
    return pl.pallas_call(
        pick_body,
        out_shape=jax.ShapeDtypeStruct((count, w_rate.shape[0]), BF16),
        in_specs=[VMEM],
        out_specs=VMEM,
        compiler_params=params(4),
        name="pick",
    )(w_rate.T)


def load_body(from_ref, out_ref, sem):
    copy = pltpu.make_async_copy(from_ref, out_ref, sem)
    copy.start()
    copy.wait()


def load(array):
    return pl.pallas_call(
        load_body,
        out_shape=jax.ShapeDtypeStruct(array.shape, array.dtype),
        in_specs=[pl.BlockSpec(memory_space=pl.ANY)],
        out_specs=VMEM,
        scratch_shapes=[pltpu.SemaphoreType.DMA],
        compiler_params=params(6),
        cost_estimate=cost(0, 2 * array.size),
        name="load",
    )(pltpu.with_memory_space_constraint(array, pltpu.HBM))


def add_body(left_ref, right_ref, out_ref):
    out_ref[...] = left_ref[...] + right_ref[...]


def add(left, right):
    return pl.pallas_call(
        add_body,
        out_shape=jax.ShapeDtypeStruct(left.shape, left.dtype),
        in_specs=[VMEM] * 2,
        out_specs=VMEM,
        compiler_params=params(4),
        name="add",
    )(left, right)


def rms(field):
    return field * lax.rsqrt(jnp.mean(field * field, axis=-1, keepdims=True) + epsilon)


def project_body(count, heads, size, factor, *refs):
    pieces = refs[:count]
    w_ref, w_rate_ref, bias_ref, q_ref, k_ref, v_ref, rate_ref = refs[count:]
    rows = jnp.concatenate([piece[...] for piece in pieces], axis=0)
    logits = lax.dot_general(
        rows, w_rate_ref[...], (((1,), (1,)), ((), ())), preferred_element_type=F32
    )
    lanes = rate_ref.shape[1]
    rate_ref[...] = jax.nn.softplus(logits[:, :lanes] + bias_ref[...].reshape(1, lanes)) * factor
    projected = jnp.dot(rows, w_ref[...], preferred_element_type=F32)
    for head in range(heads):
        base = 3 * size * head
        query = projected[:, base : base + size].astype(BF16).astype(F32)
        key = projected[:, base + size : base + 2 * size].astype(BF16).astype(F32)
        q_ref[head] = rms(query).astype(BF16)
        k_ref[head] = rms(key).astype(BF16)
        v_ref[head] = projected[:, base + 2 * size : base + 3 * size].astype(BF16)


def project(pieces, w, w_rate, bias, heads, size, factor):
    rows, width = pieces[0].shape
    total = rows * len(pieces)
    columns = w.shape[1]
    lanes = 3 * heads
    return pl.pallas_call(
        functools.partial(project_body, len(pieces), heads, size, factor),
        out_shape=[jax.ShapeDtypeStruct((heads, total, size), BF16)] * 3
        + [jax.ShapeDtypeStruct((total, lanes), F32)],
        in_specs=[VMEM] * (len(pieces) + 3),
        out_specs=[VMEM] * 4,
        compiler_params=params(-(-6 * total * width // MB)),
        cost_estimate=cost(2 * total * width * columns, width * columns * 2),
        name="project",
    )(*pieces, w, w_rate, bias)


LANES = 128


def packing(part, size):
    full, rest = divmod(size, LANES)
    if rest not in (0, LANES // 2):
        raise ValueError("head size")
    half = -(-part // 32) * 16 if rest else 0
    return full, half, full * part + half


def lower_rows(array, rows):
    missing = rows - array.shape[0]
    if not missing:
        return array
    return jnp.concatenate([array, jnp.zeros((missing, array.shape[1]), array.dtype)], axis=0)


def pack(rows, out_ref):
    part, size = rows.shape
    full, half, _ = packing(part, size)
    kind = out_ref.dtype
    for j in range(full):
        out_ref[j * part : (j + 1) * part, :] = rows[:, j * LANES : (j + 1) * LANES].astype(kind)
    if half:
        rest = rows[:, full * LANES :]
        tail = jnp.concatenate([rest[:half], lower_rows(rest[half:], half)], axis=1)
        out_ref[full * part :, :] = tail.astype(kind)


def stack_rows(refs, full_ref, me, part):
    full, half, _ = packing(part, full_ref.shape[1])
    for k, ref in enumerate(refs):
        at = pl.multiple_of((me ^ k) * part, part)
        for j in range(full):
            full_ref[pl.ds(at, part), j * LANES : (j + 1) * LANES] = ref[
                j * part : (j + 1) * part, :
            ]
        if half:
            tail = ref[full * part :, :]
            low = part - half
            full_ref[pl.ds(at, half), full * LANES :] = tail[:, : LANES // 2]
            full_ref[pl.ds(at + half, low), full * LANES :] = tail[:low, LANES // 2 :]


def joined(refs, head=None):
    return jnp.concatenate([ref[...] if head is None else ref[head] for ref in refs], axis=0)


def update_body(n, head, size, chunks, fresh, *refs):
    me = lax.axis_index("tokens").astype(jnp.int32)
    kvr = refs[: 3 * chunks]
    refs = refs[3 * chunks :]
    many = 3 if fresh else n
    weights = refs[:many]
    refs = refs[many:]
    outs = refs[:n]
    full_ref, delta_ref = refs[-2:]
    part = full_ref.shape[0] // n
    if fresh:
        for i in range(3):
            matrix = weights[i][head]
            full_ref[i * size : (i + 1) * size, :] = matrix.astype(BF16)
            delta_ref[i * size : (i + 1) * size, :] = matrix
        pack(delta_ref[pl.ds(pl.multiple_of(me * part, part), part), :], refs[n])
    else:
        stack_rows(weights, full_ref, me, part)
    gate = full_ref[:size, :]
    lift = full_ref[size : 2 * size, :]
    down = full_ref[2 * size :, :]
    key = joined(kvr[0::3], head)
    value = joined(kvr[1::3], head)
    rate = joined(kvr[2::3])[:, 3 * head : 3 * head + 3]
    key32 = key.astype(F32)
    gate_pre = jnp.dot(key, gate, preferred_element_type=F32)
    lift_pre = jnp.dot(key, lift, preferred_element_type=F32)
    hidden_grad = lax.dot_general(
        value, down, (((1,), (1,)), ((), ())), preferred_element_type=F32
    )
    sig = jax.nn.sigmoid(gate_pre)
    activated = gate_pre * sig
    hidden = (activated * lift_pre).astype(BF16)
    gate_grad = (hidden_grad * lift_pre * sig * (1.0 + gate_pre * (1.0 - sig))).astype(BF16)
    lift_grad = (hidden_grad * activated).astype(BF16)
    key_gate = (key32 * rate[:, 0:1]).astype(BF16)
    key_lift = (key32 * rate[:, 1:2]).astype(BF16)
    hidden_rate = (hidden.astype(F32) * rate[:, 2:3]).astype(BF16)
    pairs = ((key_gate, gate_grad), (key_lift, lift_grad), (hidden_rate, value))
    for i, (left, right) in enumerate(pairs):
        delta_ref[i * size : (i + 1) * size, :] = lax.dot_general(
            left, right, (((0,), (0,)), ((), ())), preferred_element_type=F32
        )
    for k in range(n):
        pack(delta_ref[pl.ds(pl.multiple_of((me ^ k) * part, part), part), :], outs[k])


def update(kvr, weights, n, head, size, fresh):
    flat = [a for group in kvr for a in group]
    total = 3 * size
    rows = packing(total // n, size)[2]
    outs = [jax.ShapeDtypeStruct((rows, LANES), F32)] + [
        jax.ShapeDtypeStruct((rows, LANES), BF16)
    ] * (n - 1)
    if fresh:
        outs.append(outs[0])
    args = flat + list(weights)
    tokens = sum(g[2].shape[0] for g in kvr)
    return pl.pallas_call(
        functools.partial(update_body, n, head, size, len(kvr), fresh),
        out_shape=outs,
        in_specs=[VMEM] * len(args),
        out_specs=[VMEM] * len(outs),
        scratch_shapes=[pltpu.VMEM((total, size), BF16), pltpu.VMEM((total, size), F32)],
        compiler_params=params(-(-64 * tokens * size // MB)),
        cost_estimate=cost(2e9 * tokens / 384, 4e6),
        name="update",
    )(*args)


def renorm_body(n, part, size, *refs):
    old_ref, round_ref = refs[n : n + 2]
    full, half, _ = packing(part, size)
    delta = refs[0][...]
    for ref in refs[1:n]:
        delta = delta + ref[...].astype(F32)
    old = old_ref[...]
    summed = old + delta
    upper = lax.broadcasted_iota(jnp.int32, (half, LANES), 1) < LANES // 2 if half else None

    def row_scale(field):
        square = field * field
        total = sum(
            jnp.sum(square[j * part : (j + 1) * part], axis=-1, keepdims=True) for j in range(full)
        )
        if half:
            tail = square[full * part :]
            high = jnp.sum(jnp.where(upper, tail, 0.0), axis=-1, keepdims=True)
            low = jnp.sum(jnp.where(upper, 0.0, tail), axis=-1, keepdims=True)
            total = total + jnp.concatenate([high, low[: part - half]], axis=0)
        return total / size + epsilon

    factor = jnp.sqrt(row_scale(old)) * lax.rsqrt(row_scale(summed))
    news = [summed[j * part : (j + 1) * part] * factor for j in range(full)]
    if half:
        both = jnp.where(upper, factor[:half], lower_rows(factor[half:], half))
        news.append(summed[full * part :] * both)
    new = jnp.concatenate(news, axis=0)
    round_ref[...] = new.astype(BF16)
    if len(refs) > n + 2:
        refs[n + 2][...] = new


def renorm(parts, old, part, size, keep):
    args = list(parts) + [old]
    outs = [jax.ShapeDtypeStruct(old.shape, BF16)]
    if keep:
        outs.append(jax.ShapeDtypeStruct(old.shape, F32))
    return pl.pallas_call(
        functools.partial(renorm_body, len(parts), part, size),
        out_shape=outs,
        in_specs=[VMEM] * len(args),
        out_specs=[VMEM] * len(outs),
        compiler_params=params(4),
        cost_estimate=cost(1e6, 2e6),
        name="renorm",
    )(*args)


def head_gain(gain_ref, head, size):
    return gain_ref[...].reshape(1, -1)[:, head * size : (head + 1) * size]


def fast_rows(query, full_ref, size, gain):
    gate = full_ref[:size, :]
    lift = full_ref[size : 2 * size, :]
    down = full_ref[2 * size :, :]
    query_gate = jnp.dot(query, gate, preferred_element_type=F32)
    query_lift = jnp.dot(query, lift, preferred_element_type=F32)
    hidden = (query_gate * jax.nn.sigmoid(query_gate) * query_lift).astype(BF16)
    fast = jnp.dot(hidden, down, preferred_element_type=F32)
    return (rms(fast) * gain).astype(BF16)


def answer_body(n, head, chunks, *refs):
    me = lax.axis_index("tokens").astype(jnp.int32)
    queries = refs[:chunks]
    weights = refs[chunks : chunks + n]
    gain_ref, out_ref, full_ref = refs[chunks + n :]
    size = full_ref.shape[1]
    stack_rows(weights, full_ref, me, full_ref.shape[0] // n)
    out_ref[...] = fast_rows(
        joined(queries, head), full_ref, size, head_gain(gain_ref, head, size)
    )


def answer(queries, weights, gain, n, head, size):
    tokens = sum(q.shape[1] for q in queries)
    args = list(queries) + list(weights) + [gain]
    return pl.pallas_call(
        functools.partial(answer_body, n, head, len(queries)),
        out_shape=jax.ShapeDtypeStruct((tokens, size), BF16),
        in_specs=[VMEM] * len(args),
        out_specs=VMEM,
        scratch_shapes=[pltpu.VMEM((3 * size, size), BF16)],
        compiler_params=params(-(-64 * tokens * size // MB)),
        cost_estimate=cost(1e9 * tokens / 384, 2e6),
        name="answer",
    )(*args)


def finish_body(n, head, chunks, places, block, others, chained, *refs):
    me = lax.axis_index("tokens").astype(jnp.int32)
    origin = sources()
    queries = refs[:chunks]
    refs = refs[chunks:]
    weights = refs[:n]
    gain_ref = refs[n]
    before = refs[n + 1 : n + 1 + others]
    refs = refs[n + 1 + others + (1 if chained else 0) :]
    out_ref, full_ref, rows_ref, sem = refs
    size = full_ref.shape[1]
    stack_rows(weights, full_ref, me, full_ref.shape[0] // n)
    piece = rows_ref.shape[0] // places
    normed = fast_rows(joined(queries, head), full_ref, size, head_gain(gain_ref, head, size))
    wide = jnp.concatenate([ref[...] for ref in before] + [normed], axis=1)
    for place in range(places):
        at = pl.multiple_of(origin[place] * piece, piece)
        rows_ref[pl.ds(at, piece), :] = wide[place * piece : (place + 1) * piece, :]
    copy = pltpu.make_async_copy(rows_ref, out_ref.at[block], sem)
    copy.start()
    copy.wait()


def finish(queries, weights, gain, n, head, size, others, places, block, blocks, before):
    tokens = sum(q.shape[1] for q in queries)
    width = size * (len(others) + 1)
    args = list(queries) + list(weights) + [gain] + list(others)
    specs = [VMEM] * len(args)
    alias = {}
    if before is not None:
        alias = {len(args): 0}
        args.append(before)
        specs.append(pl.BlockSpec(memory_space=pl.ANY))
    return pl.pallas_call(
        functools.partial(
            finish_body, n, head, len(queries), places, block, len(others), before is not None
        ),
        out_shape=jax.ShapeDtypeStruct((blocks, tokens, width), BF16),
        in_specs=specs,
        out_specs=pl.BlockSpec(memory_space=pl.ANY),
        scratch_shapes=[
            pltpu.VMEM((3 * size, size), BF16),
            pltpu.VMEM((tokens, width), BF16),
            pltpu.SemaphoreType.DMA,
        ],
        input_output_aliases=alias,
        compiler_params=params(-(-64 * tokens * size // MB)),
        cost_estimate=cost(1e9 * tokens / 384, 2e6),
        name="finish",
    )(*args)


def chips(pairs):
    return [(2 * a + c, 2 * b + c) for a, b in pairs for c in (0, 1)]


def shift(array, pairs):
    return lax.ppermute(array, "tensor", pairs)


def gather(rows):
    n = lax.axis_size("tensor")
    side = [(t, t ^ 1) for t in range(n)]
    outer = n // 2
    if outer == 4:
        first = shift(rows, chips([(1, 0), (3, 1), (0, 2), (2, 3)]))
        ends = shift(first, chips([(1, 0), (2, 3)]))
        mids = shift(rows, chips([(1, 2), (2, 1)]))
        last = shift(rows, chips([(2, 0), (0, 1), (3, 2), (1, 3)]))
        second = add(ends, mids)
        got = [rows, first, last, second]
    else:
        got = [rows] + [
            shift(rows, chips([(z, (z + k) % outer) for z in range(outer)]))
            for k in range(1, outer)
        ]
    pieces = []
    for piece in got:
        pieces += [piece, shift(piece, side)]
    return pieces


def sources():
    n = lax.axis_size("tensor")
    mine = lax.axis_index("tensor").astype(jnp.int32)
    outer = n // 2
    chip, core = mine // 2, mine % 2
    if outer == 4:
        high, low = chip // 2, chip % 2
        first = jnp.where(high == 0, 1 + 2 * low, 2 * low)
        last = jnp.where(high == 0, 2 - 2 * low, 3 - 2 * low)
        chip_of = [chip, first, last, 3 - chip]
    else:
        chip_of = [(chip + outer - k) % outer for k in range(outer)]
    found = []
    for c in chip_of:
        found += [c * 2 + core, c * 2 + (1 - core)]
    return found


def swap(array, k):
    n = lax.axis_size("tokens")
    return lax.ppermute(array, "tokens", [(t, t ^ k) for t in range(n)])


def local(codes, scales, w_qkv, w_rate, rate_bias, fast_gate, fast_lift, fast_down, out_gain):
    blocks = codes.shape[0]
    heads, size = fast_gate.shape[:2]
    n = lax.axis_size("tokens")
    tokens = codes.shape[1] * lax.axis_size("tensor")
    factor = rate_base / math.sqrt(tokens * n)
    rate_rows = pick(w_rate, 3 * heads)
    w_qkv = load(w_qkv)
    fresh = [fast_gate, fast_lift, fast_down]
    state = [None] * heads
    weights = [fresh] * heads

    rows = []
    for block in range(blocks):
        rows.append(decode(codes, scales, block))
    out = None
    for block in range(blocks):
        pieces = gather(rows[block])
        chunks = []
        cuts = (0, -2) if block == 0 else (0, 2, -2)
        groups = [pieces[a:b] for a, b in zip(cuts, cuts[1:] + (None,))]
        for group in groups:
            chunks.append(project(group, w_qkv, rate_rows, rate_bias, heads, size, factor))
        kvr = [c[1:4] for c in chunks]
        queries = [c[0] for c in chunks]
        done = []
        for head in range(heads):
            deltas = update(kvr, weights[head], n, head, size, block == 0)
            if block == 0:
                state[head] = deltas[n]
            parts = [deltas[0]] + [swap(deltas[k], k) for k in range(1, n)]
            rounded, *kept = renorm(parts, state[head], 3 * size // n, size, block < blocks - 1)
            state[head] = kept[0] if kept else None
            weights[head] = [rounded] + [swap(rounded, k) for k in range(1, n)]
            if head < heads - 1:
                done.append(answer(queries, weights[head], out_gain, n, head, size))
            else:
                out = finish(
                    queries, weights[head], out_gain, n, head, size, done, len(pieces), block,
                    blocks, out,
                )
    return out


def solution(mesh):
    return jax.shard_map(
        local,
        mesh=mesh,
        in_specs=(
            P(None, ("tokens", "tensor"), None),
            P(None, ("tokens", "tensor"), None),
            P(None, "tensor"),
            P(),
            P("tensor"),
            P("tensor", None, None),
            P("tensor", None, None),
            P("tensor", None, None),
            P("tensor"),
        ),
        out_specs=P(None, "tokens", "tensor"),
        check_vma=False,
    )
```

```python
import functools
import math

import jax
import jax.numpy as jnp
from jax import lax
from jax.experimental import pallas as pl
from jax.experimental.pallas import tpu as pltpu
from jax.sharding import PartitionSpec as P


epsilon = 1e-06
rate_base = 0.15
F32 = jnp.float32
BF16 = jnp.bfloat16
MB = 1 << 20


VMEM = pl.BlockSpec(memory_space=pltpu.VMEM)


def params(limit):
    return pltpu.CompilerParams(vmem_limit_bytes=limit * MB)


def cost(flops, nbytes):
    return pl.CostEstimate(flops=int(flops), bytes_accessed=int(nbytes), transcendentals=0)


def decode_body(block, steps, codes_hbm, scales_hbm, out_ref, codes_ref, scales_ref, sem):
    cols = out_ref.shape[1] // steps
    groups = cols // 32
    copies = [
        pltpu.make_async_copy(scales_hbm.at[block], scales_ref, sem.at[steps]),
    ]
    for i in range(steps):
        part = pl.ds(i * cols, cols)
        copies.append(
            pltpu.make_async_copy(codes_hbm.at[block, :, part], codes_ref.at[:, part], sem.at[i])
        )
    for copy in copies:
        copy.start()
    lane = lax.broadcasted_iota(jnp.int32, (groups, cols), 1) // 32
    row = lax.broadcasted_iota(jnp.int32, (groups, cols), 0)
    spread = jnp.where(lane == row, 1.0, 0.0).astype(BF16)
    copies[0].wait()
    scales = scales_ref[...]
    power = jnp.left_shift(jnp.ones_like(scales), scales - 119).astype(F32) * (1.0 / 131072.0)
    power = power.astype(BF16)
    for i in range(steps):
        copies[1 + i].wait()
        factor = jnp.dot(
            power[:, i * groups : (i + 1) * groups], spread, preferred_element_type=F32
        )
        codes = codes_ref[:, i * cols : (i + 1) * cols]
        lower = codes & 127
        exponent = lower >> 3
        mantissa = lower & 7
        significand = jnp.where(exponent == 0, mantissa, mantissa + 8)
        whole = jnp.left_shift(significand, jnp.maximum(exponent, 1) - 1)
        signed = jnp.where(codes >= 128, -whole, whole)
        out_ref[:, i * cols : (i + 1) * cols] = (signed.astype(F32) * factor).astype(BF16)


def decode(codes, scales, block):
    rows, width = codes.shape[1:]
    steps = 4
    hbm = pl.BlockSpec(memory_space=pl.ANY)
    return pl.pallas_call(
        functools.partial(decode_body, block, steps),
        out_shape=jax.ShapeDtypeStruct((rows, width), BF16),
        in_specs=[hbm, hbm],
        out_specs=VMEM,
        scratch_shapes=[
            pltpu.VMEM((rows, width), jnp.int32),
            pltpu.VMEM((rows, scales.shape[2]), jnp.int32),
            pltpu.SemaphoreType.DMA((steps + 1,)),
        ],
        compiler_params=params(4),
        cost_estimate=cost(2e7, rows * width * 6),
        name="decode",
    )(
        pltpu.with_memory_space_constraint(codes, pltpu.HBM),
        pltpu.with_memory_space_constraint(scales, pltpu.HBM),
    )


def pick_body(rows_ref, out_ref):
    count = out_ref.shape[0]
    first = lax.axis_index("tensor") * (rows_ref.shape[0] // lax.axis_size("tensor"))
    row = lax.broadcasted_iota(jnp.int32, (count, rows_ref.shape[0]), 0) + first
    column = lax.broadcasted_iota(jnp.int32, (count, rows_ref.shape[0]), 1)
    hot = jnp.where(row == column, 1.0, 0.0).astype(BF16)
    out_ref[...] = jnp.dot(hot, rows_ref[...], preferred_element_type=F32).astype(BF16)


def pick(w_rate, lanes):
    count = -(-lanes // 16) * 16
    return pl.pallas_call(
        pick_body,
        out_shape=jax.ShapeDtypeStruct((count, w_rate.shape[0]), BF16),
        in_specs=[VMEM],
        out_specs=VMEM,
        compiler_params=params(4),
        name="pick",
    )(w_rate.T)


def load_body(from_ref, out_ref, sem):
    copy = pltpu.make_async_copy(from_ref, out_ref, sem)
    copy.start()
    copy.wait()


def load(array):
    return pl.pallas_call(
        load_body,
        out_shape=jax.ShapeDtypeStruct(array.shape, array.dtype),
        in_specs=[pl.BlockSpec(memory_space=pl.ANY)],
        out_specs=VMEM,
        scratch_shapes=[pltpu.SemaphoreType.DMA],
        compiler_params=params(6),
        cost_estimate=cost(0, 2 * array.size),
        name="load",
    )(pltpu.with_memory_space_constraint(array, pltpu.HBM))


def add_body(left_ref, right_ref, out_ref):
    out_ref[...] = left_ref[...] + right_ref[...]


def add(left, right):
    return pl.pallas_call(
        add_body,
        out_shape=jax.ShapeDtypeStruct(left.shape, left.dtype),
        in_specs=[VMEM] * 2,
        out_specs=VMEM,
        compiler_params=params(4),
        name="add",
    )(left, right)


LANES = 128


def joined(refs, head=None):
    if head is None:
        return jnp.concatenate([ref[...] for ref in refs], axis=0)
    return jnp.concatenate([ref[min(head, ref.shape[0] - 1)] for ref in refs], axis=0)


def rms(field):
    return field * lax.rsqrt(jnp.mean(field * field, axis=-1, keepdims=True) + epsilon)


def rates_of(rows, w_rate_ref, bias_ref, rate_ref, factor):
    logits = lax.dot_general(
        rows, w_rate_ref[...], (((1,), (1,)), ((), ())), preferred_element_type=F32
    )
    lanes = rate_ref.shape[1]
    rate_ref[...] = jax.nn.softplus(logits[:, :lanes] + bias_ref[...].reshape(1, lanes)) * factor


def unit_rows(field):
    return rms(field.astype(BF16).astype(F32)).astype(BF16)


def project_body(count, heads, size, factor, blocks, *refs):
    pieces = refs[:count]
    w_ref, w_rate_ref, bias_ref, q_ref, k_ref, v_ref, rate_ref, all_ref = refs[count:]
    rows = joined(pieces)
    rates_of(rows, w_rate_ref, bias_ref, rate_ref, factor)
    columns = w_ref.shape[1] // blocks

    def step(i, _):
        at = pl.ds(pl.multiple_of(i * columns, LANES), columns) if blocks > 1 else slice(None)
        all_ref[:, at] = jnp.dot(rows, w_ref[:, at], preferred_element_type=F32)
        return 0

    if blocks > 1:
        lax.fori_loop(0, blocks, step, 0)
    else:
        step(0, 0)
    for head in range(heads):
        base = 3 * size * head
        q_ref[head] = unit_rows(all_ref[:, base : base + size])
        k_ref[head] = unit_rows(all_ref[:, base + size : base + 2 * size])
        v_ref[head] = all_ref[:, base + 2 * size : base + 3 * size].astype(BF16)


def project(pieces, w, w_rate, bias, heads, size, factor):
    rows, width = pieces[0].shape
    total = rows * len(pieces)
    columns = w.shape[1]
    lanes = 3 * heads
    blocks = 1 if columns % (3 * LANES) else 3
    return pl.pallas_call(
        functools.partial(project_body, len(pieces), heads, size, factor, blocks),
        out_shape=[jax.ShapeDtypeStruct((heads, total, size), BF16)] * 3
        + [jax.ShapeDtypeStruct((total, lanes), F32)],
        in_specs=[VMEM] * (len(pieces) + 3),
        out_specs=[VMEM] * 4,
        scratch_shapes=[pltpu.VMEM((total, columns), F32)],
        compiler_params=params(-(-8 * total * width // MB)),
        cost_estimate=cost(2 * total * width * columns, width * columns * 2),
        name="project",
    )(*pieces, w, w_rate, bias)


def columns_of(rows, w_ref, start, stop):
    low = start // LANES * LANES
    high = min(-(-stop // LANES) * LANES, w_ref.shape[1])
    field = jnp.dot(rows, w_ref[:, low:high], preferred_element_type=F32)
    return field[:, start - low : stop - low]


def pair_body(count, head, size, factor, *refs):
    rows = joined(refs[:count])
    w_ref, w_rate_ref, bias_ref, k_ref, v_ref = refs[count : count + 5]
    base = 3 * size * head + size
    both = columns_of(rows, w_ref, base, base + 2 * size)
    k_ref[0] = unit_rows(both[:, :size])
    v_ref[0] = both[:, size:].astype(BF16)
    if head == 0:
        rates_of(rows, w_rate_ref, bias_ref, refs[-1], factor)


def pair(pieces, w, w_rate, bias, head, heads, size, factor):
    rows, width = pieces[0].shape
    total = rows * len(pieces)
    outs = [jax.ShapeDtypeStruct((1, total, size), BF16)] * 2
    if head == 0:
        outs.append(jax.ShapeDtypeStruct((total, 3 * heads), F32))
    return pl.pallas_call(
        functools.partial(pair_body, len(pieces), head, size, factor),
        out_shape=outs,
        in_specs=[VMEM] * (len(pieces) + 3),
        out_specs=[VMEM] * len(outs),
        compiler_params=params(-(-8 * total * width // MB)),
        cost_estimate=cost(4 * total * width * size, width * size * 4),
        name="pair",
    )(*pieces, w, w_rate, bias)


def ask_body(count, heads, size, *refs):
    rows = joined(refs[:count])
    w_ref, q_ref = refs[count:]
    for head in range(heads):
        base = 3 * size * head
        q_ref[head] = unit_rows(columns_of(rows, w_ref, base, base + size))


def ask(pieces, w, heads, size):
    rows, width = pieces[0].shape
    total = rows * len(pieces)
    return pl.pallas_call(
        functools.partial(ask_body, len(pieces), heads, size),
        out_shape=jax.ShapeDtypeStruct((heads, total, size), BF16),
        in_specs=[VMEM] * (len(pieces) + 1),
        out_specs=VMEM,
        compiler_params=params(-(-8 * total * width // MB)),
        cost_estimate=cost(2 * total * width * size * heads, width * size * 4),
        name="ask",
    )(*pieces, w)


def packing(part, size):
    full, rest = divmod(size, LANES)
    if rest not in (0, LANES // 2):
        raise ValueError("head size")
    half = -(-part // 32) * 16 if rest else 0
    return full, half, full * part + half


def lower_rows(array, rows):
    missing = rows - array.shape[0]
    if not missing:
        return array
    return jnp.concatenate([array, jnp.zeros((missing, array.shape[1]), array.dtype)], axis=0)


def pack(rows, out_ref):
    part, size = rows.shape
    full, half, _ = packing(part, size)
    kind = out_ref.dtype
    for j in range(full):
        out_ref[j * part : (j + 1) * part, :] = rows[:, j * LANES : (j + 1) * LANES].astype(kind)
    if half:
        rest = rows[:, full * LANES :]
        tail = jnp.concatenate([rest[:half], lower_rows(rest[half:], half)], axis=1)
        out_ref[full * part :, :] = tail.astype(kind)


def stack_rows(refs, full_ref, me, part):
    full, half, _ = packing(part, full_ref.shape[1])
    for k, ref in enumerate(refs):
        at = pl.multiple_of((me ^ k) * part, part)
        for j in range(full):
            full_ref[pl.ds(at, part), j * LANES : (j + 1) * LANES] = ref[
                j * part : (j + 1) * part, :
            ]
        if half:
            tail = ref[full * part :, :]
            low = part - half
            full_ref[pl.ds(at, half), full * LANES :] = tail[:, : LANES // 2]
            full_ref[pl.ds(at + half, low), full * LANES :] = tail[:low, LANES // 2 :]


def update_body(n, head, size, chunks, fresh, *refs):
    me = lax.axis_index("tokens").astype(jnp.int32)
    kvr = refs[: 3 * chunks]
    refs = refs[3 * chunks :]
    many = 3 if fresh else n
    weights = refs[:many]
    refs = refs[many:]
    outs = refs[:n]
    full_ref, delta_ref = refs[-2:]
    part = full_ref.shape[0] // n
    if fresh:
        for i in range(3):
            matrix = weights[i][head]
            full_ref[i * size : (i + 1) * size, :] = matrix.astype(BF16)
            delta_ref[i * size : (i + 1) * size, :] = matrix
        pack(delta_ref[pl.ds(pl.multiple_of(me * part, part), part), :], refs[n])
    else:
        stack_rows(weights, full_ref, me, part)
    gate = full_ref[:size, :]
    lift = full_ref[size : 2 * size, :]
    down = full_ref[2 * size :, :]
    key = joined(kvr[0::3], head)
    value = joined(kvr[1::3], head)
    rate = joined(kvr[2::3])[:, 3 * head : 3 * head + 3]
    key32 = key.astype(F32)
    gate_pre = jnp.dot(key, gate, preferred_element_type=F32)
    lift_pre = jnp.dot(key, lift, preferred_element_type=F32)
    hidden_grad = lax.dot_general(
        value, down, (((1,), (1,)), ((), ())), preferred_element_type=F32
    )
    sig = jax.nn.sigmoid(gate_pre)
    activated = gate_pre * sig
    hidden = (activated * lift_pre).astype(BF16)
    gate_grad = (hidden_grad * lift_pre * sig * (1.0 + gate_pre * (1.0 - sig))).astype(BF16)
    lift_grad = (hidden_grad * activated).astype(BF16)
    key_gate = (key32 * rate[:, 0:1]).astype(BF16)
    key_lift = (key32 * rate[:, 1:2]).astype(BF16)
    hidden_rate = (hidden.astype(F32) * rate[:, 2:3]).astype(BF16)
    pairs = ((key_gate, gate_grad), (key_lift, lift_grad), (hidden_rate, value))
    for i, (left, right) in enumerate(pairs):
        delta_ref[i * size : (i + 1) * size, :] = lax.dot_general(
            left, right, (((0,), (0,)), ((), ())), preferred_element_type=F32
        )
    for k in range(n):
        pack(delta_ref[pl.ds(pl.multiple_of((me ^ k) * part, part), part), :], outs[k])


def update(kvr, weights, n, head, size, fresh):
    flat = [a for group in kvr for a in group]
    total = 3 * size
    rows = packing(total // n, size)[2]
    outs = [jax.ShapeDtypeStruct((rows, LANES), F32)] + [
        jax.ShapeDtypeStruct((rows, LANES), BF16)
    ] * (n - 1)
    if fresh:
        outs.append(outs[0])
    args = flat + list(weights)
    tokens = sum(g[2].shape[0] for g in kvr)
    return pl.pallas_call(
        functools.partial(update_body, n, head, size, len(kvr), fresh),
        out_shape=outs,
        in_specs=[VMEM] * len(args),
        out_specs=[VMEM] * len(outs),
        scratch_shapes=[pltpu.VMEM((total, size), BF16), pltpu.VMEM((total, size), F32)],
        compiler_params=params(-(-64 * tokens * size // MB)),
        cost_estimate=cost(2e9 * tokens / 384, 4e6),
        name="update",
    )(*args)


def renorm_body(n, part, size, *refs):
    old_ref, round_ref = refs[n : n + 2]
    full, half, _ = packing(part, size)
    delta = refs[0][...]
    for ref in refs[1:n]:
        delta = delta + ref[...].astype(F32)
    old = old_ref[...]
    summed = old + delta
    upper = lax.broadcasted_iota(jnp.int32, (half, LANES), 1) < LANES // 2 if half else None

    def row_scale(field):
        square = field * field
        total = sum(
            jnp.sum(square[j * part : (j + 1) * part], axis=-1, keepdims=True) for j in range(full)
        )
        if half:
            tail = square[full * part :]
            high = jnp.sum(jnp.where(upper, tail, 0.0), axis=-1, keepdims=True)
            low = jnp.sum(jnp.where(upper, 0.0, tail), axis=-1, keepdims=True)
            total = total + jnp.concatenate([high, low[: part - half]], axis=0)
        return total / size + epsilon

    factor = jnp.sqrt(row_scale(old)) * lax.rsqrt(row_scale(summed))
    news = [summed[j * part : (j + 1) * part] * factor for j in range(full)]
    if half:
        both = jnp.where(upper, factor[:half], lower_rows(factor[half:], half))
        news.append(summed[full * part :] * both)
    new = jnp.concatenate(news, axis=0)
    round_ref[...] = new.astype(BF16)
    if len(refs) > n + 2:
        refs[n + 2][...] = new


def renorm(parts, old, part, size, keep):
    args = list(parts) + [old]
    outs = [jax.ShapeDtypeStruct(old.shape, BF16)]
    if keep:
        outs.append(jax.ShapeDtypeStruct(old.shape, F32))
    return pl.pallas_call(
        functools.partial(renorm_body, len(parts), part, size),
        out_shape=outs,
        in_specs=[VMEM] * len(args),
        out_specs=[VMEM] * len(outs),
        compiler_params=params(4),
        cost_estimate=cost(1e6, 2e6),
        name="renorm",
    )(*args)


def head_gain(gain_ref, head, size):
    return gain_ref[...].reshape(1, -1)[:, head * size : (head + 1) * size]


def fast_rows(query, full_ref, size, gain):
    gate = full_ref[:size, :]
    lift = full_ref[size : 2 * size, :]
    down = full_ref[2 * size :, :]
    query_gate = jnp.dot(query, gate, preferred_element_type=F32)
    query_lift = jnp.dot(query, lift, preferred_element_type=F32)
    hidden = (query_gate * jax.nn.sigmoid(query_gate) * query_lift).astype(BF16)
    fast = jnp.dot(hidden, down, preferred_element_type=F32)
    return (rms(fast) * gain).astype(BF16)


def answer_body(n, head, chunks, *refs):
    me = lax.axis_index("tokens").astype(jnp.int32)
    queries = refs[:chunks]
    weights = refs[chunks : chunks + n]
    gain_ref, out_ref, full_ref = refs[chunks + n :]
    size = full_ref.shape[1]
    stack_rows(weights, full_ref, me, full_ref.shape[0] // n)
    out_ref[...] = fast_rows(
        joined(queries, head), full_ref, size, head_gain(gain_ref, head, size)
    )


def answer(queries, weights, gain, n, head, size):
    tokens = sum(q.shape[1] for q in queries)
    args = list(queries) + list(weights) + [gain]
    return pl.pallas_call(
        functools.partial(answer_body, n, head, len(queries)),
        out_shape=jax.ShapeDtypeStruct((tokens, size), BF16),
        in_specs=[VMEM] * len(args),
        out_specs=VMEM,
        scratch_shapes=[pltpu.VMEM((3 * size, size), BF16)],
        compiler_params=params(-(-64 * tokens * size // MB)),
        cost_estimate=cost(1e9 * tokens / 384, 2e6),
        name="answer",
    )(*args)


def finish_body(n, head, chunks, places, block, others, chained, *refs):
    me = lax.axis_index("tokens").astype(jnp.int32)
    origin = sources()
    queries = refs[:chunks]
    refs = refs[chunks:]
    weights = refs[:n]
    gain_ref = refs[n]
    before = refs[n + 1 : n + 1 + others]
    refs = refs[n + 1 + others + (1 if chained else 0) :]
    out_ref, full_ref, rows_ref, sem = refs
    size = full_ref.shape[1]
    stack_rows(weights, full_ref, me, full_ref.shape[0] // n)
    piece = rows_ref.shape[0] // places
    normed = fast_rows(joined(queries, head), full_ref, size, head_gain(gain_ref, head, size))
    wide = jnp.concatenate([ref[...] for ref in before] + [normed], axis=1)
    for place in range(places):
        at = pl.multiple_of(origin[place] * piece, piece)
        rows_ref[pl.ds(at, piece), :] = wide[place * piece : (place + 1) * piece, :]
    copy = pltpu.make_async_copy(rows_ref, out_ref.at[block], sem)
    copy.start()
    copy.wait()


def finish(queries, weights, gain, n, head, size, others, places, block, blocks, before):
    tokens = sum(q.shape[1] for q in queries)
    width = size * (len(others) + 1)
    args = list(queries) + list(weights) + [gain] + list(others)
    specs = [VMEM] * len(args)
    alias = {}
    if before is not None:
        alias = {len(args): 0}
        args.append(before)
        specs.append(pl.BlockSpec(memory_space=pl.ANY))
    return pl.pallas_call(
        functools.partial(
            finish_body, n, head, len(queries), places, block, len(others), before is not None
        ),
        out_shape=jax.ShapeDtypeStruct((blocks, tokens, width), BF16),
        in_specs=specs,
        out_specs=pl.BlockSpec(memory_space=pl.ANY),
        scratch_shapes=[
            pltpu.VMEM((3 * size, size), BF16),
            pltpu.VMEM((tokens, width), BF16),
            pltpu.SemaphoreType.DMA,
        ],
        input_output_aliases=alias,
        compiler_params=params(-(-64 * tokens * size // MB)),
        cost_estimate=cost(1e9 * tokens / 384, 2e6),
        name="finish",
    )(*args)


def chips(pairs):
    return [(2 * a + c, 2 * b + c) for a, b in pairs for c in (0, 1)]


def shift(array, pairs):
    return lax.ppermute(array, "tensor", pairs)


def gather(rows):
    n = lax.axis_size("tensor")
    side = [(t, t ^ 1) for t in range(n)]
    outer = n // 2
    if outer == 4:
        first = shift(rows, chips([(1, 0), (3, 1), (0, 2), (2, 3)]))
        ends = shift(first, chips([(1, 0), (2, 3)]))
        mids = shift(rows, chips([(1, 2), (2, 1)]))
        last = shift(rows, chips([(2, 0), (0, 1), (3, 2), (1, 3)]))
        second = add(ends, mids)
        got = [rows, first, last, second]
    else:
        got = [rows] + [
            shift(rows, chips([(z, (z + k) % outer) for z in range(outer)]))
            for k in range(1, outer)
        ]
    pieces = []
    for piece in got:
        pieces += [piece, shift(piece, side)]
    return pieces


def sources():
    n = lax.axis_size("tensor")
    mine = lax.axis_index("tensor").astype(jnp.int32)
    outer = n // 2
    chip, core = mine // 2, mine % 2
    if outer == 4:
        high, low = chip // 2, chip % 2
        first = jnp.where(high == 0, 1 + 2 * low, 2 * low)
        last = jnp.where(high == 0, 2 - 2 * low, 3 - 2 * low)
        chip_of = [chip, first, last, 3 - chip]
    else:
        chip_of = [(chip + outer - k) % outer for k in range(outer)]
    found = []
    for c in chip_of:
        found += [c * 2 + core, c * 2 + (1 - core)]
    return found


def swap(array, k):
    n = lax.axis_size("tokens")
    return lax.ppermute(array, "tokens", [(t, t ^ k) for t in range(n)])


def local(codes, scales, w_qkv, w_rate, rate_bias, fast_gate, fast_lift, fast_down, out_gain):
    blocks = codes.shape[0]
    heads, size = fast_gate.shape[:2]
    n = lax.axis_size("tokens")
    tokens = codes.shape[1] * lax.axis_size("tensor")
    factor = rate_base / math.sqrt(tokens * n)
    rate_rows = pick(w_rate, 3 * heads)
    w_qkv = load(w_qkv)
    fresh = [fast_gate, fast_lift, fast_down]
    state = [None] * heads
    weights = [fresh] * heads

    rows = []
    for block in range(blocks):
        rows.append(decode(codes, scales, block))
    out = None
    for block in range(blocks):
        pieces = gather(rows[block])
        chunks = []
        final = block == blocks - 1
        cuts = (0, -2) if block == 0 else (0, 2, -2)
        groups = [pieces[a:b] for a, b in zip(cuts, cuts[1:] + (None,))]
        late = groups.pop() if final else None
        for group in groups:
            chunks.append(project(group, w_qkv, rate_rows, rate_bias, heads, size, factor))
        queries = [c[0] for c in chunks]
        if final:
            queries.append(ask(late, w_qkv, heads, size))
        done = []
        for head in range(heads):
            kvr = [c[1:4] for c in chunks]
            if final:
                found = pair(late, w_qkv, rate_rows, rate_bias, head, heads, size, factor)
                late_rates = found[2] if head == 0 else late_rates
                kvr.append((found[0], found[1], late_rates))
            deltas = update(kvr, weights[head], n, head, size, block == 0)
            if block == 0:
                state[head] = deltas[n]
            parts = [deltas[0]] + [swap(deltas[k], k) for k in range(1, n)]
            rounded, *kept = renorm(parts, state[head], 3 * size // n, size, block < blocks - 1)
            state[head] = kept[0] if kept else None
            weights[head] = [rounded] + [swap(rounded, k) for k in range(1, n)]
            if head < heads - 1:
                done.append(answer(queries, weights[head], out_gain, n, head, size))
            else:
                out = finish(
                    queries, weights[head], out_gain, n, head, size, done, len(pieces), block,
                    blocks, out,
                )
    return out


def solution(mesh):
    return jax.shard_map(
        local,
        mesh=mesh,
        in_specs=(
            P(None, ("tokens", "tensor"), None),
            P(None, ("tokens", "tensor"), None),
            P(None, "tensor"),
            P(),
            P("tensor"),
            P("tensor", None, None),
            P("tensor", None, None),
            P("tensor", None, None),
            P("tensor"),
        ),
        out_specs=P(None, "tokens", "tensor"),
        check_vma=False,
    )
```

```python
import functools
import math

import jax
import jax.numpy as jnp
from jax import lax
from jax.experimental import pallas as pl
from jax.experimental.pallas import tpu as pltpu
from jax.sharding import PartitionSpec as P


epsilon = 1e-06
rate_base = 0.15
F32 = jnp.float32
BF16 = jnp.bfloat16
MB = 1 << 20


VMEM = pl.BlockSpec(memory_space=pltpu.VMEM)


def params(limit):
    return pltpu.CompilerParams(vmem_limit_bytes=limit * MB)


def cost(flops, nbytes):
    return pl.CostEstimate(flops=int(flops), bytes_accessed=int(nbytes), transcendentals=0)


def decode_body(block, steps, codes_hbm, scales_hbm, out_ref, codes_ref, scales_ref, sem):
    cols = out_ref.shape[1] // steps
    groups = cols // 32
    copies = [
        pltpu.make_async_copy(scales_hbm.at[block], scales_ref, sem.at[steps]),
    ]
    for i in range(steps):
        part = pl.ds(i * cols, cols)
        copies.append(
            pltpu.make_async_copy(codes_hbm.at[block, :, part], codes_ref.at[:, part], sem.at[i])
        )
    for copy in copies:
        copy.start()
    lane = lax.broadcasted_iota(jnp.int32, (groups, cols), 1) // 32
    row = lax.broadcasted_iota(jnp.int32, (groups, cols), 0)
    spread = jnp.where(lane == row, 1.0, 0.0).astype(BF16)
    copies[0].wait()
    scales = scales_ref[...]
    power = jnp.left_shift(jnp.ones_like(scales), scales - 119).astype(F32) * (1.0 / 131072.0)
    power = power.astype(BF16)
    for i in range(steps):
        copies[1 + i].wait()
        factor = jnp.dot(
            power[:, i * groups : (i + 1) * groups], spread, preferred_element_type=F32
        )
        codes = codes_ref[:, i * cols : (i + 1) * cols]
        lower = codes & 127
        exponent = lower >> 3
        mantissa = lower & 7
        significand = jnp.where(exponent == 0, mantissa, mantissa + 8)
        whole = jnp.left_shift(significand, jnp.maximum(exponent, 1) - 1)
        signed = jnp.where(codes >= 128, -whole, whole)
        out_ref[:, i * cols : (i + 1) * cols] = (signed.astype(F32) * factor).astype(BF16)


def decode(codes, scales, block):
    rows, width = codes.shape[1:]
    steps = 4
    hbm = pl.BlockSpec(memory_space=pl.ANY)
    return pl.pallas_call(
        functools.partial(decode_body, block, steps),
        out_shape=jax.ShapeDtypeStruct((rows, width), BF16),
        in_specs=[hbm, hbm],
        out_specs=VMEM,
        scratch_shapes=[
            pltpu.VMEM((rows, width), jnp.int32),
            pltpu.VMEM((rows, scales.shape[2]), jnp.int32),
            pltpu.SemaphoreType.DMA((steps + 1,)),
        ],
        compiler_params=params(4),
        cost_estimate=cost(2e7, rows * width * 6),
        name="decode",
    )(
        pltpu.with_memory_space_constraint(codes, pltpu.HBM),
        pltpu.with_memory_space_constraint(scales, pltpu.HBM),
    )


def pick_body(rows_ref, out_ref):
    count = out_ref.shape[0]
    first = lax.axis_index("tensor") * (rows_ref.shape[0] // lax.axis_size("tensor"))
    row = lax.broadcasted_iota(jnp.int32, (count, rows_ref.shape[0]), 0) + first
    column = lax.broadcasted_iota(jnp.int32, (count, rows_ref.shape[0]), 1)
    hot = jnp.where(row == column, 1.0, 0.0).astype(BF16)
    out_ref[...] = jnp.dot(hot, rows_ref[...], preferred_element_type=F32).astype(BF16)


def pick(w_rate, lanes):
    count = -(-lanes // 16) * 16
    return pl.pallas_call(
        pick_body,
        out_shape=jax.ShapeDtypeStruct((count, w_rate.shape[0]), BF16),
        in_specs=[VMEM],
        out_specs=VMEM,
        compiler_params=params(4),
        name="pick",
    )(w_rate.T)


def load_body(from_ref, out_ref, sem):
    copy = pltpu.make_async_copy(from_ref, out_ref, sem)
    copy.start()
    copy.wait()


def load(array):
    return pl.pallas_call(
        load_body,
        out_shape=jax.ShapeDtypeStruct(array.shape, array.dtype),
        in_specs=[pl.BlockSpec(memory_space=pl.ANY)],
        out_specs=VMEM,
        scratch_shapes=[pltpu.SemaphoreType.DMA],
        compiler_params=params(6),
        cost_estimate=cost(0, 2 * array.size),
        name="load",
    )(pltpu.with_memory_space_constraint(array, pltpu.HBM))


def add_body(left_ref, right_ref, out_ref):
    out_ref[...] = left_ref[...] + right_ref[...]


def add(left, right):
    return pl.pallas_call(
        add_body,
        out_shape=jax.ShapeDtypeStruct(left.shape, left.dtype),
        in_specs=[VMEM] * 2,
        out_specs=VMEM,
        compiler_params=params(4),
        name="add",
    )(left, right)


LANES = 128


def joined(refs, head=None):
    if head is None:
        return jnp.concatenate([ref[...] for ref in refs], axis=0)
    return jnp.concatenate([ref[min(head, ref.shape[0] - 1)] for ref in refs], axis=0)


def rms(field):
    return field * lax.rsqrt(jnp.mean(field * field, axis=-1, keepdims=True) + epsilon)


def rates_of(rows, w_rate_ref, bias_ref, rate_ref, factor):
    logits = lax.dot_general(
        rows, w_rate_ref[...], (((1,), (1,)), ((), ())), preferred_element_type=F32
    )
    lanes = rate_ref.shape[1]
    rate_ref[...] = jax.nn.softplus(logits[:, :lanes] + bias_ref[...].reshape(1, lanes)) * factor


def unit_rows(field):
    return rms(field.astype(BF16).astype(F32)).astype(BF16)


def project_body(count, heads, size, factor, blocks, *refs):
    pieces = refs[:count]
    w_ref, w_rate_ref, bias_ref, q_ref, k_ref, v_ref, rate_ref, all_ref = refs[count:]
    rows = joined(pieces)
    rates_of(rows, w_rate_ref, bias_ref, rate_ref, factor)
    columns = w_ref.shape[1] // blocks

    def step(i, _):
        at = pl.ds(pl.multiple_of(i * columns, LANES), columns) if blocks > 1 else slice(None)
        all_ref[:, at] = jnp.dot(rows, w_ref[:, at], preferred_element_type=F32)
        return 0

    if blocks > 1:
        lax.fori_loop(0, blocks, step, 0)
    else:
        step(0, 0)
    for head in range(heads):
        base = 3 * size * head
        q_ref[head] = unit_rows(all_ref[:, base : base + size])
        k_ref[head] = unit_rows(all_ref[:, base + size : base + 2 * size])
        v_ref[head] = all_ref[:, base + 2 * size : base + 3 * size].astype(BF16)


def project(pieces, w, w_rate, bias, heads, size, factor, loop):
    rows, width = pieces[0].shape
    total = rows * len(pieces)
    columns = w.shape[1]
    lanes = 3 * heads
    blocks = 3 if loop and columns % (3 * LANES) == 0 else 1
    return pl.pallas_call(
        functools.partial(project_body, len(pieces), heads, size, factor, blocks),
        out_shape=[jax.ShapeDtypeStruct((heads, total, size), BF16)] * 3
        + [jax.ShapeDtypeStruct((total, lanes), F32)],
        in_specs=[VMEM] * (len(pieces) + 3),
        out_specs=[VMEM] * 4,
        scratch_shapes=[pltpu.VMEM((total, columns), F32)],
        compiler_params=params(-(-8 * total * width // MB)),
        cost_estimate=cost(2 * total * width * columns, width * columns * 2),
        name="project",
    )(*pieces, w, w_rate, bias)


def columns_of(rows, w_ref, start, stop):
    low = start // LANES * LANES
    high = min(-(-stop // LANES) * LANES, w_ref.shape[1])
    field = jnp.dot(rows, w_ref[:, low:high], preferred_element_type=F32)
    return field[:, start - low : stop - low]


def pair_body(count, head, size, factor, *refs):
    rows = joined(refs[:count])
    w_ref, w_rate_ref, bias_ref, k_ref, v_ref = refs[count : count + 5]
    base = 3 * size * head + size
    both = columns_of(rows, w_ref, base, base + 2 * size)
    k_ref[0] = unit_rows(both[:, :size])
    v_ref[0] = both[:, size:].astype(BF16)
    if head == 0:
        rates_of(rows, w_rate_ref, bias_ref, refs[-1], factor)


def pair(pieces, w, w_rate, bias, head, heads, size, factor):
    rows, width = pieces[0].shape
    total = rows * len(pieces)
    outs = [jax.ShapeDtypeStruct((1, total, size), BF16)] * 2
    if head == 0:
        outs.append(jax.ShapeDtypeStruct((total, 3 * heads), F32))
    return pl.pallas_call(
        functools.partial(pair_body, len(pieces), head, size, factor),
        out_shape=outs,
        in_specs=[VMEM] * (len(pieces) + 3),
        out_specs=[VMEM] * len(outs),
        compiler_params=params(-(-8 * total * width // MB)),
        cost_estimate=cost(4 * total * width * size, width * size * 4),
        name="pair",
    )(*pieces, w, w_rate, bias)


def ask_body(count, heads, size, *refs):
    rows = joined(refs[:count])
    w_ref, q_ref = refs[count:]
    for head in range(heads):
        base = 3 * size * head
        q_ref[head] = unit_rows(columns_of(rows, w_ref, base, base + size))


def ask(pieces, w, heads, size):
    rows, width = pieces[0].shape
    total = rows * len(pieces)
    return pl.pallas_call(
        functools.partial(ask_body, len(pieces), heads, size),
        out_shape=jax.ShapeDtypeStruct((heads, total, size), BF16),
        in_specs=[VMEM] * (len(pieces) + 1),
        out_specs=VMEM,
        compiler_params=params(-(-8 * total * width // MB)),
        cost_estimate=cost(2 * total * width * size * heads, width * size * 4),
        name="ask",
    )(*pieces, w)


def packing(part, size):
    full, rest = divmod(size, LANES)
    if rest not in (0, LANES // 2):
        raise ValueError("head size")
    half = -(-part // 32) * 16 if rest else 0
    return full, half, full * part + half


def lower_rows(array, rows):
    missing = rows - array.shape[0]
    if not missing:
        return array
    return jnp.concatenate([array, jnp.zeros((missing, array.shape[1]), array.dtype)], axis=0)


def pack(rows, out_ref):
    part, size = rows.shape
    full, half, _ = packing(part, size)
    kind = out_ref.dtype
    for j in range(full):
        out_ref[j * part : (j + 1) * part, :] = rows[:, j * LANES : (j + 1) * LANES].astype(kind)
    if half:
        rest = rows[:, full * LANES :]
        tail = jnp.concatenate([rest[:half], lower_rows(rest[half:], half)], axis=1)
        out_ref[full * part :, :] = tail.astype(kind)


def stack_rows(refs, full_ref, me, part):
    full, half, _ = packing(part, full_ref.shape[1])
    for k, ref in enumerate(refs):
        at = pl.multiple_of((me ^ k) * part, part)
        for j in range(full):
            full_ref[pl.ds(at, part), j * LANES : (j + 1) * LANES] = ref[
                j * part : (j + 1) * part, :
            ]
        if half:
            tail = ref[full * part :, :]
            low = part - half
            full_ref[pl.ds(at, half), full * LANES :] = tail[:, : LANES // 2]
            full_ref[pl.ds(at + half, low), full * LANES :] = tail[:low, LANES // 2 :]


def update_body(n, head, size, chunks, fresh, *refs):
    me = lax.axis_index("tokens").astype(jnp.int32)
    kvr = refs[: 3 * chunks]
    refs = refs[3 * chunks :]
    many = 3 if fresh else n
    weights = refs[:many]
    refs = refs[many:]
    outs = refs[:n]
    full_ref, delta_ref = refs[-2:]
    part = full_ref.shape[0] // n
    if fresh:
        for i in range(3):
            matrix = weights[i][head]
            full_ref[i * size : (i + 1) * size, :] = matrix.astype(BF16)
            delta_ref[i * size : (i + 1) * size, :] = matrix
        pack(delta_ref[pl.ds(pl.multiple_of(me * part, part), part), :], refs[n])
    else:
        stack_rows(weights, full_ref, me, part)
    gate = full_ref[:size, :]
    lift = full_ref[size : 2 * size, :]
    down = full_ref[2 * size :, :]
    key = joined(kvr[0::3], head)
    value = joined(kvr[1::3], head)
    rate = joined(kvr[2::3])[:, 3 * head : 3 * head + 3]
    key32 = key.astype(F32)
    gate_pre = jnp.dot(key, gate, preferred_element_type=F32)
    lift_pre = jnp.dot(key, lift, preferred_element_type=F32)
    hidden_grad = lax.dot_general(
        value, down, (((1,), (1,)), ((), ())), preferred_element_type=F32
    )
    sig = jax.nn.sigmoid(gate_pre)
    activated = gate_pre * sig
    hidden = (activated * lift_pre).astype(BF16)
    gate_grad = (hidden_grad * lift_pre * sig * (1.0 + gate_pre * (1.0 - sig))).astype(BF16)
    lift_grad = (hidden_grad * activated).astype(BF16)
    key_gate = (key32 * rate[:, 0:1]).astype(BF16)
    key_lift = (key32 * rate[:, 1:2]).astype(BF16)
    hidden_rate = (hidden.astype(F32) * rate[:, 2:3]).astype(BF16)
    pairs = ((key_gate, gate_grad), (key_lift, lift_grad), (hidden_rate, value))
    for i, (left, right) in enumerate(pairs):
        delta_ref[i * size : (i + 1) * size, :] = lax.dot_general(
            left, right, (((0,), (0,)), ((), ())), preferred_element_type=F32
        )
    for k in range(n):
        pack(delta_ref[pl.ds(pl.multiple_of((me ^ k) * part, part), part), :], outs[k])


def update(kvr, weights, n, head, size, fresh):
    flat = [a for group in kvr for a in group]
    total = 3 * size
    rows = packing(total // n, size)[2]
    outs = [jax.ShapeDtypeStruct((rows, LANES), F32)] + [
        jax.ShapeDtypeStruct((rows, LANES), BF16)
    ] * (n - 1)
    if fresh:
        outs.append(outs[0])
    args = flat + list(weights)
    tokens = sum(g[2].shape[0] for g in kvr)
    return pl.pallas_call(
        functools.partial(update_body, n, head, size, len(kvr), fresh),
        out_shape=outs,
        in_specs=[VMEM] * len(args),
        out_specs=[VMEM] * len(outs),
        scratch_shapes=[pltpu.VMEM((total, size), BF16), pltpu.VMEM((total, size), F32)],
        compiler_params=params(-(-64 * tokens * size // MB)),
        cost_estimate=cost(2e9 * tokens / 384, 4e6),
        name="update",
    )(*args)


def renorm_body(n, part, size, *refs):
    old_ref, round_ref = refs[n : n + 2]
    full, half, _ = packing(part, size)
    delta = refs[0][...]
    for ref in refs[1:n]:
        delta = delta + ref[...].astype(F32)
    old = old_ref[...]
    summed = old + delta
    upper = lax.broadcasted_iota(jnp.int32, (half, LANES), 1) < LANES // 2 if half else None

    def row_scale(field):
        square = field * field
        total = sum(
            jnp.sum(square[j * part : (j + 1) * part], axis=-1, keepdims=True) for j in range(full)
        )
        if half:
            tail = square[full * part :]
            high = jnp.sum(jnp.where(upper, tail, 0.0), axis=-1, keepdims=True)
            low = jnp.sum(jnp.where(upper, 0.0, tail), axis=-1, keepdims=True)
            total = total + jnp.concatenate([high, low[: part - half]], axis=0)
        return total / size + epsilon

    factor = jnp.sqrt(row_scale(old)) * lax.rsqrt(row_scale(summed))
    news = [summed[j * part : (j + 1) * part] * factor for j in range(full)]
    if half:
        both = jnp.where(upper, factor[:half], lower_rows(factor[half:], half))
        news.append(summed[full * part :] * both)
    new = jnp.concatenate(news, axis=0)
    round_ref[...] = new.astype(BF16)
    if len(refs) > n + 2:
        refs[n + 2][...] = new


def renorm(parts, old, part, size, keep):
    args = list(parts) + [old]
    outs = [jax.ShapeDtypeStruct(old.shape, BF16)]
    if keep:
        outs.append(jax.ShapeDtypeStruct(old.shape, F32))
    return pl.pallas_call(
        functools.partial(renorm_body, len(parts), part, size),
        out_shape=outs,
        in_specs=[VMEM] * len(args),
        out_specs=[VMEM] * len(outs),
        compiler_params=params(4),
        cost_estimate=cost(1e6, 2e6),
        name="renorm",
    )(*args)


def head_gain(gain_ref, head, size):
    return gain_ref[...].reshape(1, -1)[:, head * size : (head + 1) * size]


def fast_rows(query, full_ref, size, gain):
    gate = full_ref[:size, :]
    lift = full_ref[size : 2 * size, :]
    down = full_ref[2 * size :, :]
    query_gate = jnp.dot(query, gate, preferred_element_type=F32)
    query_lift = jnp.dot(query, lift, preferred_element_type=F32)
    hidden = (query_gate * jax.nn.sigmoid(query_gate) * query_lift).astype(BF16)
    fast = jnp.dot(hidden, down, preferred_element_type=F32)
    return (rms(fast) * gain).astype(BF16)


def answer_body(n, head, chunks, *refs):
    me = lax.axis_index("tokens").astype(jnp.int32)
    queries = refs[:chunks]
    weights = refs[chunks : chunks + n]
    gain_ref, out_ref, full_ref = refs[chunks + n :]
    size = full_ref.shape[1]
    stack_rows(weights, full_ref, me, full_ref.shape[0] // n)
    out_ref[...] = fast_rows(
        joined(queries, head), full_ref, size, head_gain(gain_ref, head, size)
    )


def answer(queries, weights, gain, n, head, size):
    tokens = sum(q.shape[1] for q in queries)
    args = list(queries) + list(weights) + [gain]
    return pl.pallas_call(
        functools.partial(answer_body, n, head, len(queries)),
        out_shape=jax.ShapeDtypeStruct((tokens, size), BF16),
        in_specs=[VMEM] * len(args),
        out_specs=VMEM,
        scratch_shapes=[pltpu.VMEM((3 * size, size), BF16)],
        compiler_params=params(-(-64 * tokens * size // MB)),
        cost_estimate=cost(1e9 * tokens / 384, 2e6),
        name="answer",
    )(*args)


def finish_body(n, head, chunks, places, block, others, chained, *refs):
    me = lax.axis_index("tokens").astype(jnp.int32)
    origin = sources()
    queries = refs[:chunks]
    refs = refs[chunks:]
    weights = refs[:n]
    gain_ref = refs[n]
    before = refs[n + 1 : n + 1 + others]
    refs = refs[n + 1 + others + (1 if chained else 0) :]
    out_ref, full_ref, rows_ref, sem = refs
    size = full_ref.shape[1]
    stack_rows(weights, full_ref, me, full_ref.shape[0] // n)
    piece = rows_ref.shape[0] // places
    normed = fast_rows(joined(queries, head), full_ref, size, head_gain(gain_ref, head, size))
    wide = jnp.concatenate([ref[...] for ref in before] + [normed], axis=1)
    for place in range(places):
        at = pl.multiple_of(origin[place] * piece, piece)
        rows_ref[pl.ds(at, piece), :] = wide[place * piece : (place + 1) * piece, :]
    copy = pltpu.make_async_copy(rows_ref, out_ref.at[block], sem)
    copy.start()
    copy.wait()


def finish(queries, weights, gain, n, head, size, others, places, block, blocks, before):
    tokens = sum(q.shape[1] for q in queries)
    width = size * (len(others) + 1)
    args = list(queries) + list(weights) + [gain] + list(others)
    specs = [VMEM] * len(args)
    alias = {}
    if before is not None:
        alias = {len(args): 0}
        args.append(before)
        specs.append(pl.BlockSpec(memory_space=pl.ANY))
    return pl.pallas_call(
        functools.partial(
            finish_body, n, head, len(queries), places, block, len(others), before is not None
        ),
        out_shape=jax.ShapeDtypeStruct((blocks, tokens, width), BF16),
        in_specs=specs,
        out_specs=pl.BlockSpec(memory_space=pl.ANY),
        scratch_shapes=[
            pltpu.VMEM((3 * size, size), BF16),
            pltpu.VMEM((tokens, width), BF16),
            pltpu.SemaphoreType.DMA,
        ],
        input_output_aliases=alias,
        compiler_params=params(-(-64 * tokens * size // MB)),
        cost_estimate=cost(1e9 * tokens / 384, 2e6),
        name="finish",
    )(*args)


def chips(pairs):
    return [(2 * a + c, 2 * b + c) for a, b in pairs for c in (0, 1)]


def shift(array, pairs):
    return lax.ppermute(array, "tensor", pairs)


def gather(rows):
    n = lax.axis_size("tensor")
    side = [(t, t ^ 1) for t in range(n)]
    outer = n // 2
    if outer == 4:
        first = shift(rows, chips([(1, 0), (3, 1), (0, 2), (2, 3)]))
        ends = shift(first, chips([(1, 0), (2, 3)]))
        mids = shift(rows, chips([(1, 2), (2, 1)]))
        last = shift(rows, chips([(2, 0), (0, 1), (3, 2), (1, 3)]))
        second = add(ends, mids)
        got = [rows, first, last, second]
    else:
        got = [rows] + [
            shift(rows, chips([(z, (z + k) % outer) for z in range(outer)]))
            for k in range(1, outer)
        ]
    pieces = []
    for piece in got:
        pieces += [piece, shift(piece, side)]
    return pieces


def sources():
    n = lax.axis_size("tensor")
    mine = lax.axis_index("tensor").astype(jnp.int32)
    outer = n // 2
    chip, core = mine // 2, mine % 2
    if outer == 4:
        high, low = chip // 2, chip % 2
        first = jnp.where(high == 0, 1 + 2 * low, 2 * low)
        last = jnp.where(high == 0, 2 - 2 * low, 3 - 2 * low)
        chip_of = [chip, first, last, 3 - chip]
    else:
        chip_of = [(chip + outer - k) % outer for k in range(outer)]
    found = []
    for c in chip_of:
        found += [c * 2 + core, c * 2 + (1 - core)]
    return found


def swap(array, k):
    n = lax.axis_size("tokens")
    return lax.ppermute(array, "tokens", [(t, t ^ k) for t in range(n)])


def local(codes, scales, w_qkv, w_rate, rate_bias, fast_gate, fast_lift, fast_down, out_gain):
    blocks = codes.shape[0]
    heads, size = fast_gate.shape[:2]
    n = lax.axis_size("tokens")
    tokens = codes.shape[1] * lax.axis_size("tensor")
    factor = rate_base / math.sqrt(tokens * n)
    rate_rows = pick(w_rate, 3 * heads)
    w_qkv = load(w_qkv)
    fresh = [fast_gate, fast_lift, fast_down]
    state = [None] * heads
    weights = [fresh] * heads

    rows = []
    for block in range(blocks):
        rows.append(decode(codes, scales, block))
    out = None
    for block in range(blocks):
        pieces = gather(rows[block])
        chunks = []
        final = block == blocks - 1
        cuts = (0, -2) if block == 0 else (0, 2, -2)
        groups = [pieces[a:b] for a, b in zip(cuts, cuts[1:] + (None,))]
        late = groups.pop() if final else None
        for i, group in enumerate(groups):
            loop = block > 0 and i == 0
            chunks.append(project(group, w_qkv, rate_rows, rate_bias, heads, size, factor, loop))
        queries = [c[0] for c in chunks]
        if final:
            queries.append(ask(late, w_qkv, heads, size))
        done = []
        for head in range(heads):
            kvr = [c[1:4] for c in chunks]
            if final:
                found = pair(late, w_qkv, rate_rows, rate_bias, head, heads, size, factor)
                late_rates = found[2] if head == 0 else late_rates
                kvr.append((found[0], found[1], late_rates))
            deltas = update(kvr, weights[head], n, head, size, block == 0)
            if block == 0:
                state[head] = deltas[n]
            parts = [deltas[0]] + [swap(deltas[k], k) for k in range(1, n)]
            rounded, *kept = renorm(parts, state[head], 3 * size // n, size, block < blocks - 1)
            state[head] = kept[0] if kept else None
            weights[head] = [rounded] + [swap(rounded, k) for k in range(1, n)]
            if head < heads - 1:
                done.append(answer(queries, weights[head], out_gain, n, head, size))
            else:
                out = finish(
                    queries, weights[head], out_gain, n, head, size, done, len(pieces), block,
                    blocks, out,
                )
    return out


def solution(mesh):
    return jax.shard_map(
        local,
        mesh=mesh,
        in_specs=(
            P(None, ("tokens", "tensor"), None),
            P(None, ("tokens", "tensor"), None),
            P(None, "tensor"),
            P(),
            P("tensor"),
            P("tensor", None, None),
            P("tensor", None, None),
            P("tensor", None, None),
            P("tensor"),
        ),
        out_specs=P(None, "tokens", "tensor"),
        check_vma=False,
    )
```

```python
import functools
import math

import jax
import jax.numpy as jnp
from jax import lax
from jax.experimental import pallas as pl
from jax.experimental.pallas import tpu as pltpu
from jax.sharding import PartitionSpec as P


epsilon = 1e-06
rate_base = 0.15
F32 = jnp.float32
BF16 = jnp.bfloat16
MB = 1 << 20


VMEM = pl.BlockSpec(memory_space=pltpu.VMEM)


def params(limit):
    return pltpu.CompilerParams(vmem_limit_bytes=limit * MB)


def cost(flops, nbytes):
    return pl.CostEstimate(flops=int(flops), bytes_accessed=int(nbytes), transcendentals=0)


def decode_body(block, steps, codes_hbm, scales_hbm, out_ref, codes_ref, scales_ref, sem):
    cols = out_ref.shape[1] // steps
    groups = cols // 32
    copies = [
        pltpu.make_async_copy(scales_hbm.at[block], scales_ref, sem.at[steps]),
    ]
    for i in range(steps):
        part = pl.ds(i * cols, cols)
        copies.append(
            pltpu.make_async_copy(codes_hbm.at[block, :, part], codes_ref.at[:, part], sem.at[i])
        )
    for copy in copies:
        copy.start()
    lane = lax.broadcasted_iota(jnp.int32, (groups, cols), 1) // 32
    row = lax.broadcasted_iota(jnp.int32, (groups, cols), 0)
    spread = jnp.where(lane == row, 1.0, 0.0).astype(BF16)
    copies[0].wait()
    scales = scales_ref[...]
    power = jnp.left_shift(jnp.ones_like(scales), scales - 119).astype(F32) * (1.0 / 131072.0)
    power = power.astype(BF16)
    for i in range(steps):
        copies[1 + i].wait()
        factor = jnp.dot(
            power[:, i * groups : (i + 1) * groups], spread, preferred_element_type=F32
        )
        codes = codes_ref[:, i * cols : (i + 1) * cols]
        lower = codes & 127
        exponent = lower >> 3
        mantissa = lower & 7
        significand = jnp.where(exponent == 0, mantissa, mantissa + 8)
        whole = jnp.left_shift(significand, jnp.maximum(exponent, 1) - 1)
        signed = jnp.where(codes >= 128, -whole, whole)
        out_ref[:, i * cols : (i + 1) * cols] = (signed.astype(F32) * factor).astype(BF16)


def decode(codes, scales, block):
    rows, width = codes.shape[1:]
    steps = 4
    hbm = pl.BlockSpec(memory_space=pl.ANY)
    return pl.pallas_call(
        functools.partial(decode_body, block, steps),
        out_shape=jax.ShapeDtypeStruct((rows, width), BF16),
        in_specs=[hbm, hbm],
        out_specs=VMEM,
        scratch_shapes=[
            pltpu.VMEM((rows, width), jnp.int32),
            pltpu.VMEM((rows, scales.shape[2]), jnp.int32),
            pltpu.SemaphoreType.DMA((steps + 1,)),
        ],
        compiler_params=params(4),
        cost_estimate=cost(2e7, rows * width * 6),
        name="decode",
    )(
        pltpu.with_memory_space_constraint(codes, pltpu.HBM),
        pltpu.with_memory_space_constraint(scales, pltpu.HBM),
    )


def pick_body(rows_ref, out_ref):
    count = out_ref.shape[0]
    first = lax.axis_index("tensor") * (rows_ref.shape[0] // lax.axis_size("tensor"))
    row = lax.broadcasted_iota(jnp.int32, (count, rows_ref.shape[0]), 0) + first
    column = lax.broadcasted_iota(jnp.int32, (count, rows_ref.shape[0]), 1)
    hot = jnp.where(row == column, 1.0, 0.0).astype(BF16)
    out_ref[...] = jnp.dot(hot, rows_ref[...], preferred_element_type=F32).astype(BF16)


def pick(w_rate, lanes):
    count = -(-lanes // 16) * 16
    return pl.pallas_call(
        pick_body,
        out_shape=jax.ShapeDtypeStruct((count, w_rate.shape[0]), BF16),
        in_specs=[VMEM],
        out_specs=VMEM,
        compiler_params=params(4),
        name="pick",
    )(w_rate.T)


def load_body(from_ref, out_ref, sem):
    copy = pltpu.make_async_copy(from_ref, out_ref, sem)
    copy.start()
    copy.wait()


def load(array):
    return pl.pallas_call(
        load_body,
        out_shape=jax.ShapeDtypeStruct(array.shape, array.dtype),
        in_specs=[pl.BlockSpec(memory_space=pl.ANY)],
        out_specs=VMEM,
        scratch_shapes=[pltpu.SemaphoreType.DMA],
        compiler_params=params(6),
        cost_estimate=cost(0, 2 * array.size),
        name="load",
    )(pltpu.with_memory_space_constraint(array, pltpu.HBM))


def add_body(left_ref, right_ref, out_ref):
    out_ref[...] = left_ref[...] + right_ref[...]


def add(left, right):
    return pl.pallas_call(
        add_body,
        out_shape=jax.ShapeDtypeStruct(left.shape, left.dtype),
        in_specs=[VMEM] * 2,
        out_specs=VMEM,
        compiler_params=params(4),
        name="add",
    )(left, right)


LANES = 128


def joined(refs, head=None):
    if head is None:
        return jnp.concatenate([ref[...] for ref in refs], axis=0)
    return jnp.concatenate([ref[min(head, ref.shape[0] - 1)] for ref in refs], axis=0)


def rms(field):
    return field * lax.rsqrt(jnp.mean(field * field, axis=-1, keepdims=True) + epsilon)


def rates_of(rows, w_rate_ref, bias_ref, rate_ref, factor):
    logits = lax.dot_general(
        rows, w_rate_ref[...], (((1,), (1,)), ((), ())), preferred_element_type=F32
    )
    lanes = rate_ref.shape[1]
    rate_ref[...] = jax.nn.softplus(logits[:, :lanes] + bias_ref[...].reshape(1, lanes)) * factor


def unit_rows(field):
    return rms(field.astype(BF16).astype(F32)).astype(BF16)


def project_body(count, heads, size, factor, blocks, *refs):
    pieces = refs[:count]
    w_ref, w_rate_ref, bias_ref, q_ref, k_ref, v_ref, rate_ref, all_ref = refs[count:]
    rows = joined(pieces)
    rates_of(rows, w_rate_ref, bias_ref, rate_ref, factor)
    columns = w_ref.shape[1] // blocks

    def step(i, _):
        at = pl.ds(pl.multiple_of(i * columns, LANES), columns) if blocks > 1 else slice(None)
        all_ref[:, at] = jnp.dot(rows, w_ref[:, at], preferred_element_type=F32)
        return 0

    if blocks > 1:
        lax.fori_loop(0, blocks, step, 0)
    else:
        step(0, 0)
    for head in range(heads):
        base = 3 * size * head
        q_ref[head] = unit_rows(all_ref[:, base : base + size])
        k_ref[head] = unit_rows(all_ref[:, base + size : base + 2 * size])
        v_ref[head] = all_ref[:, base + 2 * size : base + 3 * size].astype(BF16)


def project(pieces, w, w_rate, bias, heads, size, factor, loop):
    rows, width = pieces[0].shape
    total = rows * len(pieces)
    columns = w.shape[1]
    lanes = 3 * heads
    blocks = 3 if loop and columns % (3 * LANES) == 0 else 1
    return pl.pallas_call(
        functools.partial(project_body, len(pieces), heads, size, factor, blocks),
        out_shape=[jax.ShapeDtypeStruct((heads, total, size), BF16)] * 3
        + [jax.ShapeDtypeStruct((total, lanes), F32)],
        in_specs=[VMEM] * (len(pieces) + 3),
        out_specs=[VMEM] * 4,
        scratch_shapes=[pltpu.VMEM((total, columns), F32)],
        compiler_params=params(-(-8 * total * width // MB)),
        cost_estimate=cost(2 * total * width * columns, width * columns * 2),
        name="project",
    )(*pieces, w, w_rate, bias)


def columns_of(rows, w_ref, start, stop):
    low = start // LANES * LANES
    high = min(-(-stop // LANES) * LANES, w_ref.shape[1])
    field = jnp.dot(rows, w_ref[:, low:high], preferred_element_type=F32)
    return field[:, start - low : stop - low]


def keys_body(count, wanted, size, factor, *refs):
    rows = joined(refs[:count])
    w_ref, w_rate_ref, bias_ref, k_ref, v_ref = refs[count : count + 5]
    for place, head in enumerate(wanted):
        base = 3 * size * head + size
        both = columns_of(rows, w_ref, base, base + 2 * size)
        k_ref[place] = unit_rows(both[:, :size])
        v_ref[place] = both[:, size:].astype(BF16)
    if wanted[0] == 0:
        rates_of(rows, w_rate_ref, bias_ref, refs[-1], factor)


def keys(pieces, w, w_rate, bias, wanted, heads, size, factor):
    rows, width = pieces[0].shape
    total = rows * len(pieces)
    outs = [jax.ShapeDtypeStruct((len(wanted), total, size), BF16)] * 2
    if wanted[0] == 0:
        outs.append(jax.ShapeDtypeStruct((total, 3 * heads), F32))
    return pl.pallas_call(
        functools.partial(keys_body, len(pieces), wanted, size, factor),
        out_shape=outs,
        in_specs=[VMEM] * (len(pieces) + 3),
        out_specs=[VMEM] * len(outs),
        compiler_params=params(-(-8 * total * width // MB)),
        cost_estimate=cost(4 * total * width * size * len(wanted), 4 * width * size * len(wanted)),
        name="keys",
    )(*pieces, w, w_rate, bias)


def ask_body(count, heads, size, *refs):
    rows = joined(refs[:count])
    w_ref, q_ref = refs[count:]
    for head in range(heads):
        base = 3 * size * head
        q_ref[head] = unit_rows(columns_of(rows, w_ref, base, base + size))


def ask(pieces, w, heads, size):
    rows, width = pieces[0].shape
    total = rows * len(pieces)
    return pl.pallas_call(
        functools.partial(ask_body, len(pieces), heads, size),
        out_shape=jax.ShapeDtypeStruct((heads, total, size), BF16),
        in_specs=[VMEM] * (len(pieces) + 1),
        out_specs=VMEM,
        compiler_params=params(-(-8 * total * width // MB)),
        cost_estimate=cost(2 * total * width * size * heads, width * size * 4),
        name="ask",
    )(*pieces, w)


def packing(part, size):
    full, rest = divmod(size, LANES)
    if rest not in (0, LANES // 2):
        raise ValueError("head size")
    half = -(-part // 32) * 16 if rest else 0
    return full, half, full * part + half


def lower_rows(array, rows):
    missing = rows - array.shape[0]
    if not missing:
        return array
    return jnp.concatenate([array, jnp.zeros((missing, array.shape[1]), array.dtype)], axis=0)


def pack(rows, out_ref):
    part, size = rows.shape
    full, half, _ = packing(part, size)
    kind = out_ref.dtype
    for j in range(full):
        out_ref[j * part : (j + 1) * part, :] = rows[:, j * LANES : (j + 1) * LANES].astype(kind)
    if half:
        rest = rows[:, full * LANES :]
        tail = jnp.concatenate([rest[:half], lower_rows(rest[half:], half)], axis=1)
        out_ref[full * part :, :] = tail.astype(kind)


def stack_rows(refs, full_ref, me, part):
    full, half, _ = packing(part, full_ref.shape[1])
    for k, ref in enumerate(refs):
        at = pl.multiple_of((me ^ k) * part, part)
        for j in range(full):
            full_ref[pl.ds(at, part), j * LANES : (j + 1) * LANES] = ref[
                j * part : (j + 1) * part, :
            ]
        if half:
            tail = ref[full * part :, :]
            low = part - half
            full_ref[pl.ds(at, half), full * LANES :] = tail[:, : LANES // 2]
            full_ref[pl.ds(at + half, low), full * LANES :] = tail[:low, LANES // 2 :]


def update_body(n, head, size, chunks, fresh, *refs):
    me = lax.axis_index("tokens").astype(jnp.int32)
    kvr = refs[: 3 * chunks]
    refs = refs[3 * chunks :]
    many = 3 if fresh else n
    weights = refs[:many]
    refs = refs[many:]
    outs = refs[:n]
    full_ref, delta_ref = refs[-2:]
    part = full_ref.shape[0] // n
    if fresh:
        for i in range(3):
            matrix = weights[i][head]
            full_ref[i * size : (i + 1) * size, :] = matrix.astype(BF16)
            delta_ref[i * size : (i + 1) * size, :] = matrix
        pack(delta_ref[pl.ds(pl.multiple_of(me * part, part), part), :], refs[n])
    else:
        stack_rows(weights, full_ref, me, part)
    gate = full_ref[:size, :]
    lift = full_ref[size : 2 * size, :]
    down = full_ref[2 * size :, :]
    key = joined(kvr[0::3], head)
    value = joined(kvr[1::3], head)
    rate = joined(kvr[2::3])[:, 3 * head : 3 * head + 3]
    key32 = key.astype(F32)
    gate_pre = jnp.dot(key, gate, preferred_element_type=F32)
    lift_pre = jnp.dot(key, lift, preferred_element_type=F32)
    hidden_grad = lax.dot_general(
        value, down, (((1,), (1,)), ((), ())), preferred_element_type=F32
    )
    sig = jax.nn.sigmoid(gate_pre)
    activated = gate_pre * sig
    hidden = (activated * lift_pre).astype(BF16)
    gate_grad = (hidden_grad * lift_pre * sig * (1.0 + gate_pre * (1.0 - sig))).astype(BF16)
    lift_grad = (hidden_grad * activated).astype(BF16)
    key_gate = (key32 * rate[:, 0:1]).astype(BF16)
    key_lift = (key32 * rate[:, 1:2]).astype(BF16)
    hidden_rate = (hidden.astype(F32) * rate[:, 2:3]).astype(BF16)
    pairs = ((key_gate, gate_grad), (key_lift, lift_grad), (hidden_rate, value))
    for i, (left, right) in enumerate(pairs):
        delta_ref[i * size : (i + 1) * size, :] = lax.dot_general(
            left, right, (((0,), (0,)), ((), ())), preferred_element_type=F32
        )
    for k in range(n):
        pack(delta_ref[pl.ds(pl.multiple_of((me ^ k) * part, part), part), :], outs[k])


def update(kvr, weights, n, head, size, fresh):
    flat = [a for group in kvr for a in group]
    total = 3 * size
    rows = packing(total // n, size)[2]
    outs = [jax.ShapeDtypeStruct((rows, LANES), F32)] + [
        jax.ShapeDtypeStruct((rows, LANES), BF16)
    ] * (n - 1)
    if fresh:
        outs.append(outs[0])
    args = flat + list(weights)
    tokens = sum(g[2].shape[0] for g in kvr)
    return pl.pallas_call(
        functools.partial(update_body, n, head, size, len(kvr), fresh),
        out_shape=outs,
        in_specs=[VMEM] * len(args),
        out_specs=[VMEM] * len(outs),
        scratch_shapes=[pltpu.VMEM((total, size), BF16), pltpu.VMEM((total, size), F32)],
        compiler_params=params(-(-64 * tokens * size // MB)),
        cost_estimate=cost(2e9 * tokens / 384, 4e6),
        name="update",
    )(*args)


def renorm_body(n, part, size, *refs):
    old_ref, round_ref = refs[n : n + 2]
    full, half, _ = packing(part, size)
    delta = refs[0][...]
    for ref in refs[1:n]:
        delta = delta + ref[...].astype(F32)
    old = old_ref[...]
    summed = old + delta
    upper = lax.broadcasted_iota(jnp.int32, (half, LANES), 1) < LANES // 2 if half else None

    def row_scale(field):
        square = field * field
        total = sum(
            jnp.sum(square[j * part : (j + 1) * part], axis=-1, keepdims=True) for j in range(full)
        )
        if half:
            tail = square[full * part :]
            high = jnp.sum(jnp.where(upper, tail, 0.0), axis=-1, keepdims=True)
            low = jnp.sum(jnp.where(upper, 0.0, tail), axis=-1, keepdims=True)
            total = total + jnp.concatenate([high, low[: part - half]], axis=0)
        return total / size + epsilon

    factor = jnp.sqrt(row_scale(old)) * lax.rsqrt(row_scale(summed))
    news = [summed[j * part : (j + 1) * part] * factor for j in range(full)]
    if half:
        both = jnp.where(upper, factor[:half], lower_rows(factor[half:], half))
        news.append(summed[full * part :] * both)
    new = jnp.concatenate(news, axis=0)
    round_ref[...] = new.astype(BF16)
    if len(refs) > n + 2:
        refs[n + 2][...] = new


def renorm(parts, old, part, size, keep):
    args = list(parts) + [old]
    outs = [jax.ShapeDtypeStruct(old.shape, BF16)]
    if keep:
        outs.append(jax.ShapeDtypeStruct(old.shape, F32))
    return pl.pallas_call(
        functools.partial(renorm_body, len(parts), part, size),
        out_shape=outs,
        in_specs=[VMEM] * len(args),
        out_specs=[VMEM] * len(outs),
        compiler_params=params(4),
        cost_estimate=cost(1e6, 2e6),
        name="renorm",
    )(*args)


def head_gain(gain_ref, head, size):
    return gain_ref[...].reshape(1, -1)[:, head * size : (head + 1) * size]


def fast_rows(query, full_ref, size, gain):
    gate = full_ref[:size, :]
    lift = full_ref[size : 2 * size, :]
    down = full_ref[2 * size :, :]
    query_gate = jnp.dot(query, gate, preferred_element_type=F32)
    query_lift = jnp.dot(query, lift, preferred_element_type=F32)
    hidden = (query_gate * jax.nn.sigmoid(query_gate) * query_lift).astype(BF16)
    fast = jnp.dot(hidden, down, preferred_element_type=F32)
    return (rms(fast) * gain).astype(BF16)


def answer_body(n, head, chunks, *refs):
    me = lax.axis_index("tokens").astype(jnp.int32)
    queries = refs[:chunks]
    weights = refs[chunks : chunks + n]
    gain_ref, out_ref, full_ref = refs[chunks + n :]
    size = full_ref.shape[1]
    stack_rows(weights, full_ref, me, full_ref.shape[0] // n)
    out_ref[...] = fast_rows(
        joined(queries, head), full_ref, size, head_gain(gain_ref, head, size)
    )


def answer(queries, weights, gain, n, head, size):
    tokens = sum(q.shape[1] for q in queries)
    args = list(queries) + list(weights) + [gain]
    return pl.pallas_call(
        functools.partial(answer_body, n, head, len(queries)),
        out_shape=jax.ShapeDtypeStruct((tokens, size), BF16),
        in_specs=[VMEM] * len(args),
        out_specs=VMEM,
        scratch_shapes=[pltpu.VMEM((3 * size, size), BF16)],
        compiler_params=params(-(-64 * tokens * size // MB)),
        cost_estimate=cost(1e9 * tokens / 384, 2e6),
        name="answer",
    )(*args)


def finish_body(n, head, chunks, places, block, others, chained, *refs):
    me = lax.axis_index("tokens").astype(jnp.int32)
    origin = sources()
    queries = refs[:chunks]
    refs = refs[chunks:]
    weights = refs[:n]
    gain_ref = refs[n]
    before = refs[n + 1 : n + 1 + others]
    refs = refs[n + 1 + others + (1 if chained else 0) :]
    out_ref, full_ref, rows_ref, sem = refs
    size = full_ref.shape[1]
    stack_rows(weights, full_ref, me, full_ref.shape[0] // n)
    piece = rows_ref.shape[0] // places
    query = joined(queries, head)
    gain = head_gain(gain_ref, head, size)
    step = places // 2
    copies = []
    for first in range(0, places, step):
        rows = slice(first * piece, (first + step) * piece)
        normed = fast_rows(query[rows], full_ref, size, gain)
        wide = jnp.concatenate([ref[rows, :] for ref in before] + [normed], axis=1)
        rows_ref[rows, :] = wide
        for place in range(first, first + step):
            at = pl.multiple_of(origin[place] * piece, piece)
            copies.append(
                pltpu.make_async_copy(
                    rows_ref.at[place * piece : (place + 1) * piece],
                    out_ref.at[block, pl.ds(at, piece)],
                    sem.at[place],
                )
            )
            copies[-1].start()
    for copy in copies:
        copy.wait()


def finish(queries, weights, gain, n, head, size, others, places, block, blocks, before):
    tokens = sum(q.shape[1] for q in queries)
    width = size * (len(others) + 1)
    args = list(queries) + list(weights) + [gain] + list(others)
    specs = [VMEM] * len(args)
    alias = {}
    if before is not None:
        alias = {len(args): 0}
        args.append(before)
        specs.append(pl.BlockSpec(memory_space=pl.ANY))
    return pl.pallas_call(
        functools.partial(
            finish_body, n, head, len(queries), places, block, len(others), before is not None
        ),
        out_shape=jax.ShapeDtypeStruct((blocks, tokens, width), BF16),
        in_specs=specs,
        out_specs=pl.BlockSpec(memory_space=pl.ANY),
        scratch_shapes=[
            pltpu.VMEM((3 * size, size), BF16),
            pltpu.VMEM((tokens, width), BF16),
            pltpu.SemaphoreType.DMA((places,)),
        ],
        input_output_aliases=alias,
        compiler_params=params(-(-64 * tokens * size // MB)),
        cost_estimate=cost(1e9 * tokens / 384, 2e6),
        name="finish",
    )(*args)


def chips(pairs):
    return [(2 * a + c, 2 * b + c) for a, b in pairs for c in (0, 1)]


def shift(array, pairs):
    return lax.ppermute(array, "tensor", pairs)


def gather(rows):
    n = lax.axis_size("tensor")
    side = [(t, t ^ 1) for t in range(n)]
    outer = n // 2
    if outer == 4:
        first = shift(rows, chips([(1, 0), (3, 1), (0, 2), (2, 3)]))
        ends = shift(first, chips([(1, 0), (2, 3)]))
        mids = shift(rows, chips([(1, 2), (2, 1)]))
        last = shift(rows, chips([(2, 0), (0, 1), (3, 2), (1, 3)]))
        second = add(ends, mids)
        got = [rows, first, last, second]
    else:
        got = [rows] + [
            shift(rows, chips([(z, (z + k) % outer) for z in range(outer)]))
            for k in range(1, outer)
        ]
    pieces = []
    for piece in got:
        pieces += [piece, shift(piece, side)]
    return pieces


def sources():
    n = lax.axis_size("tensor")
    mine = lax.axis_index("tensor").astype(jnp.int32)
    outer = n // 2
    chip, core = mine // 2, mine % 2
    if outer == 4:
        high, low = chip // 2, chip % 2
        first = jnp.where(high == 0, 1 + 2 * low, 2 * low)
        last = jnp.where(high == 0, 2 - 2 * low, 3 - 2 * low)
        chip_of = [chip, first, last, 3 - chip]
    else:
        chip_of = [(chip + outer - k) % outer for k in range(outer)]
    found = []
    for c in chip_of:
        found += [c * 2 + core, c * 2 + (1 - core)]
    return found


def swap(array, k):
    n = lax.axis_size("tokens")
    return lax.ppermute(array, "tokens", [(t, t ^ k) for t in range(n)])


def local(codes, scales, w_qkv, w_rate, rate_bias, fast_gate, fast_lift, fast_down, out_gain):
    blocks = codes.shape[0]
    heads, size = fast_gate.shape[:2]
    n = lax.axis_size("tokens")
    tokens = codes.shape[1] * lax.axis_size("tensor")
    factor = rate_base / math.sqrt(tokens * n)
    rate_rows = pick(w_rate, 3 * heads)
    w_qkv = load(w_qkv)
    fresh = [fast_gate, fast_lift, fast_down]
    state = [None] * heads
    weights = [fresh] * heads
    every = tuple(range(heads))

    rows = []
    for block in range(blocks):
        rows.append(decode(codes, scales, block))
    out = None
    for block in range(blocks):
        pieces = gather(rows[block])
        final = block == blocks - 1
        first = 2 if block else -2
        early, late = pieces[:first], pieces[-2:]
        given = (w_qkv, rate_rows, rate_bias)
        query, *group = project(early, *given, heads, size, factor, block > 0)
        groups = [group]
        if block:
            groups.append(keys(pieces[2:-2], *given, every, heads, size, factor))
        if not final:
            groups.append(keys(late, *given, every, heads, size, factor))
        queries = [query, ask(pieces[first:], w_qkv, heads, size)]
        done = []
        for head in range(heads):
            kvr = list(groups)
            if final:
                found = keys(late, *given, (head,), heads, size, factor)
                late_rates = found[2] if head == 0 else late_rates
                kvr.append((found[0], found[1], late_rates))
            deltas = update(kvr, weights[head], n, head, size, block == 0)
            if block == 0:
                state[head] = deltas[n]
            parts = [deltas[0]] + [swap(deltas[k], k) for k in range(1, n)]
            rounded, *kept = renorm(parts, state[head], 3 * size // n, size, block < blocks - 1)
            state[head] = kept[0] if kept else None
            weights[head] = [rounded] + [swap(rounded, k) for k in range(1, n)]
            if head < heads - 1:
                done.append(answer(queries, weights[head], out_gain, n, head, size))
            else:
                out = finish(
                    queries, weights[head], out_gain, n, head, size, done, len(pieces), block,
                    blocks, out,
                )
    return out


def solution(mesh):
    return jax.shard_map(
        local,
        mesh=mesh,
        in_specs=(
            P(None, ("tokens", "tensor"), None),
            P(None, ("tokens", "tensor"), None),
            P(None, "tensor"),
            P(),
            P("tensor"),
            P("tensor", None, None),
            P("tensor", None, None),
            P("tensor", None, None),
            P("tensor"),
        ),
        out_specs=P(None, "tokens", "tensor"),
        check_vma=False,
    )
```

```python
import functools
import math

import jax
import jax.numpy as jnp
from jax import lax
from jax.experimental import pallas as pl
from jax.experimental.pallas import tpu as pltpu
from jax.sharding import PartitionSpec as P


epsilon = 1e-06
rate_base = 0.15
F32 = jnp.float32
BF16 = jnp.bfloat16
MB = 1 << 20


VMEM = pl.BlockSpec(memory_space=pltpu.VMEM)


def params(limit):
    return pltpu.CompilerParams(vmem_limit_bytes=limit * MB)


def cost(flops, nbytes):
    return pl.CostEstimate(flops=int(flops), bytes_accessed=int(nbytes), transcendentals=0)


def decode_body(block, steps, codes_hbm, scales_hbm, out_ref, codes_ref, scales_ref, sem):
    cols = out_ref.shape[1] // steps
    groups = cols // 32
    copies = [
        pltpu.make_async_copy(scales_hbm.at[block], scales_ref, sem.at[steps]),
    ]
    for i in range(steps):
        part = pl.ds(i * cols, cols)
        copies.append(
            pltpu.make_async_copy(codes_hbm.at[block, :, part], codes_ref.at[:, part], sem.at[i])
        )
    for copy in copies:
        copy.start()
    lane = lax.broadcasted_iota(jnp.int32, (groups, cols), 1) // 32
    row = lax.broadcasted_iota(jnp.int32, (groups, cols), 0)
    spread = jnp.where(lane == row, 1.0, 0.0).astype(BF16)
    copies[0].wait()
    scales = scales_ref[...]
    power = jnp.left_shift(jnp.ones_like(scales), scales - 119).astype(F32) * (1.0 / 131072.0)
    power = power.astype(BF16)
    for i in range(steps):
        copies[1 + i].wait()
        factor = jnp.dot(
            power[:, i * groups : (i + 1) * groups], spread, preferred_element_type=F32
        )
        codes = codes_ref[:, i * cols : (i + 1) * cols]
        lower = codes & 127
        shifted = jnp.left_shift((lower & 7) | 8, (lower >> 3) - 1)
        whole = jnp.where(lower < 8, lower, shifted).astype(F32)
        signed = jnp.where(codes >= 128, -whole, whole)
        out_ref[:, i * cols : (i + 1) * cols] = (signed * factor).astype(BF16)


def decode(codes, scales, block):
    rows, width = codes.shape[1:]
    steps = 1
    hbm = pl.BlockSpec(memory_space=pl.ANY)
    return pl.pallas_call(
        functools.partial(decode_body, block, steps),
        out_shape=jax.ShapeDtypeStruct((rows, width), BF16),
        in_specs=[hbm, hbm],
        out_specs=VMEM,
        scratch_shapes=[
            pltpu.VMEM((rows, width), jnp.int32),
            pltpu.VMEM((rows, scales.shape[2]), jnp.int32),
            pltpu.SemaphoreType.DMA((steps + 1,)),
        ],
        compiler_params=params(4),
        cost_estimate=cost(2e7, rows * width * 6),
        name="decode",
    )(
        pltpu.with_memory_space_constraint(codes, pltpu.HBM),
        pltpu.with_memory_space_constraint(scales, pltpu.HBM),
    )


def pick_body(rows_ref, out_ref):
    count = out_ref.shape[0]
    first = lax.axis_index("tensor") * (rows_ref.shape[0] // lax.axis_size("tensor"))
    row = lax.broadcasted_iota(jnp.int32, (count, rows_ref.shape[0]), 0) + first
    column = lax.broadcasted_iota(jnp.int32, (count, rows_ref.shape[0]), 1)
    hot = jnp.where(row == column, 1.0, 0.0).astype(BF16)
    out_ref[...] = jnp.dot(hot, rows_ref[...], preferred_element_type=F32).astype(BF16)


def pick(w_rate, lanes):
    count = -(-lanes // 16) * 16
    return pl.pallas_call(
        pick_body,
        out_shape=jax.ShapeDtypeStruct((count, w_rate.shape[0]), BF16),
        in_specs=[VMEM],
        out_specs=VMEM,
        compiler_params=params(4),
        name="pick",
    )(w_rate.T)


def load_body(from_ref, out_ref, sem):
    copy = pltpu.make_async_copy(from_ref, out_ref, sem)
    copy.start()
    copy.wait()


def load(array):
    return pl.pallas_call(
        load_body,
        out_shape=jax.ShapeDtypeStruct(array.shape, array.dtype),
        in_specs=[pl.BlockSpec(memory_space=pl.ANY)],
        out_specs=VMEM,
        scratch_shapes=[pltpu.SemaphoreType.DMA],
        compiler_params=params(6),
        cost_estimate=cost(0, 2 * array.size),
        name="load",
    )(pltpu.with_memory_space_constraint(array, pltpu.HBM))


def add_body(left_ref, right_ref, out_ref):
    out_ref[...] = left_ref[...] + right_ref[...]


def add(left, right):
    return pl.pallas_call(
        add_body,
        out_shape=jax.ShapeDtypeStruct(left.shape, left.dtype),
        in_specs=[VMEM] * 2,
        out_specs=VMEM,
        compiler_params=params(4),
        name="add",
    )(left, right)


LANES = 128


def joined(refs, head=None):
    if head is None:
        return jnp.concatenate([ref[...] for ref in refs], axis=0)
    return jnp.concatenate([ref[min(head, ref.shape[0] - 1)] for ref in refs], axis=0)


def rms(field):
    return field * lax.rsqrt(jnp.mean(field * field, axis=-1, keepdims=True) + epsilon)


def rates_of(rows, w_rate_ref, bias_ref, rate_ref, factor):
    logits = lax.dot_general(
        rows, w_rate_ref[...], (((1,), (1,)), ((), ())), preferred_element_type=F32
    )
    lanes = rate_ref.shape[1]
    rate_ref[...] = jax.nn.softplus(logits[:, :lanes] + bias_ref[...].reshape(1, lanes)) * factor


def unit_rows(field):
    return rms(field.astype(BF16).astype(F32)).astype(BF16)


def project_body(count, heads, size, factor, blocks, *refs):
    pieces = refs[:count]
    w_ref, w_rate_ref, bias_ref, q_ref, k_ref, v_ref, rate_ref, all_ref = refs[count:]
    rows = joined(pieces)
    rates_of(rows, w_rate_ref, bias_ref, rate_ref, factor)
    columns = w_ref.shape[1] // blocks

    def step(i, _):
        at = pl.ds(pl.multiple_of(i * columns, LANES), columns) if blocks > 1 else slice(None)
        all_ref[:, at] = jnp.dot(rows, w_ref[:, at], preferred_element_type=F32)
        return 0

    if blocks > 1:
        lax.fori_loop(0, blocks, step, 0)
    else:
        step(0, 0)
    for head in range(heads):
        base = 3 * size * head
        q_ref[head] = unit_rows(all_ref[:, base : base + size])
        k_ref[head] = unit_rows(all_ref[:, base + size : base + 2 * size])
        v_ref[head] = all_ref[:, base + 2 * size : base + 3 * size].astype(BF16)


def project(pieces, w, w_rate, bias, heads, size, factor, loop):
    rows, width = pieces[0].shape
    total = rows * len(pieces)
    columns = w.shape[1]
    lanes = 3 * heads
    blocks = 3 if loop and columns % (3 * LANES) == 0 else 1
    return pl.pallas_call(
        functools.partial(project_body, len(pieces), heads, size, factor, blocks),
        out_shape=[jax.ShapeDtypeStruct((heads, total, size), BF16)] * 3
        + [jax.ShapeDtypeStruct((total, lanes), F32)],
        in_specs=[VMEM] * (len(pieces) + 3),
        out_specs=[VMEM] * 4,
        scratch_shapes=[pltpu.VMEM((total, columns), F32)],
        compiler_params=params(-(-8 * total * width // MB)),
        cost_estimate=cost(2 * total * width * columns, width * columns * 2),
        name="project",
    )(*pieces, w, w_rate, bias)


def columns_of(rows, w_ref, start, stop):
    low = start // LANES * LANES
    high = min(-(-stop // LANES) * LANES, w_ref.shape[1])
    field = jnp.dot(rows, w_ref[:, low:high], preferred_element_type=F32)
    return field[:, start - low : stop - low]


def keys_body(count, wanted, size, factor, *refs):
    rows = joined(refs[:count])
    w_ref, w_rate_ref, bias_ref, k_ref, v_ref = refs[count : count + 5]
    for place, head in enumerate(wanted):
        base = 3 * size * head + size
        both = columns_of(rows, w_ref, base, base + 2 * size)
        k_ref[place] = unit_rows(both[:, :size])
        v_ref[place] = both[:, size:].astype(BF16)
    if wanted[0] == 0:
        rates_of(rows, w_rate_ref, bias_ref, refs[-1], factor)


def keys(pieces, w, w_rate, bias, wanted, heads, size, factor):
    rows, width = pieces[0].shape
    total = rows * len(pieces)
    outs = [jax.ShapeDtypeStruct((len(wanted), total, size), BF16)] * 2
    if wanted[0] == 0:
        outs.append(jax.ShapeDtypeStruct((total, 3 * heads), F32))
    return pl.pallas_call(
        functools.partial(keys_body, len(pieces), wanted, size, factor),
        out_shape=outs,
        in_specs=[VMEM] * (len(pieces) + 3),
        out_specs=[VMEM] * len(outs),
        compiler_params=params(-(-8 * total * width // MB)),
        cost_estimate=cost(4 * total * width * size * len(wanted), 4 * width * size * len(wanted)),
        name="keys",
    )(*pieces, w, w_rate, bias)


def ask_body(count, heads, size, *refs):
    rows = joined(refs[:count])
    w_ref, q_ref = refs[count:]
    for head in range(heads):
        base = 3 * size * head
        q_ref[head] = unit_rows(columns_of(rows, w_ref, base, base + size))


def ask(pieces, w, heads, size):
    rows, width = pieces[0].shape
    total = rows * len(pieces)
    return pl.pallas_call(
        functools.partial(ask_body, len(pieces), heads, size),
        out_shape=jax.ShapeDtypeStruct((heads, total, size), BF16),
        in_specs=[VMEM] * (len(pieces) + 1),
        out_specs=VMEM,
        compiler_params=params(-(-8 * total * width // MB)),
        cost_estimate=cost(2 * total * width * size * heads, width * size * 4),
        name="ask",
    )(*pieces, w)


def packing(part, size):
    full, rest = divmod(size, LANES)
    if rest not in (0, LANES // 2):
        raise ValueError("head size")
    half = -(-part // 32) * 16 if rest else 0
    return full, half, full * part + half


def lower_rows(array, rows):
    missing = rows - array.shape[0]
    if not missing:
        return array
    return jnp.concatenate([array, jnp.zeros((missing, array.shape[1]), array.dtype)], axis=0)


def pack(rows, out_ref):
    part, size = rows.shape
    full, half, _ = packing(part, size)
    kind = out_ref.dtype
    for j in range(full):
        out_ref[j * part : (j + 1) * part, :] = rows[:, j * LANES : (j + 1) * LANES].astype(kind)
    if half:
        rest = rows[:, full * LANES :]
        tail = jnp.concatenate([rest[:half], lower_rows(rest[half:], half)], axis=1)
        out_ref[full * part :, :] = tail.astype(kind)


def stack_rows(refs, full_ref, me, part):
    full, half, _ = packing(part, full_ref.shape[1])
    for k, ref in enumerate(refs):
        at = pl.multiple_of((me ^ k) * part, part)
        for j in range(full):
            full_ref[pl.ds(at, part), j * LANES : (j + 1) * LANES] = ref[
                j * part : (j + 1) * part, :
            ]
        if half:
            tail = ref[full * part :, :]
            low = part - half
            full_ref[pl.ds(at, half), full * LANES :] = tail[:, : LANES // 2]
            full_ref[pl.ds(at + half, low), full * LANES :] = tail[:low, LANES // 2 :]


def update_body(n, head, size, chunks, fresh, *refs):
    me = lax.axis_index("tokens").astype(jnp.int32)
    kvr = refs[: 3 * chunks]
    refs = refs[3 * chunks :]
    many = 3 if fresh else n
    weights = refs[:many]
    refs = refs[many:]
    outs = refs[:n]
    full_ref, delta_ref = refs[-2:]
    part = full_ref.shape[0] // n
    if fresh:
        for i in range(3):
            matrix = weights[i][head]
            full_ref[i * size : (i + 1) * size, :] = matrix.astype(BF16)
            delta_ref[i * size : (i + 1) * size, :] = matrix
        pack(delta_ref[pl.ds(pl.multiple_of(me * part, part), part), :], refs[n])
    else:
        stack_rows(weights, full_ref, me, part)
    gate = full_ref[:size, :]
    lift = full_ref[size : 2 * size, :]
    down = full_ref[2 * size :, :]
    key = joined(kvr[0::3], head)
    value = joined(kvr[1::3], head)
    rate = joined(kvr[2::3])[:, 3 * head : 3 * head + 3]
    key32 = key.astype(F32)
    gate_pre = jnp.dot(key, gate, preferred_element_type=F32)
    lift_pre = jnp.dot(key, lift, preferred_element_type=F32)
    hidden_grad = lax.dot_general(
        value, down, (((1,), (1,)), ((), ())), preferred_element_type=F32
    )
    sig = jax.nn.sigmoid(gate_pre)
    activated = gate_pre * sig
    hidden = (activated * lift_pre).astype(BF16)
    gate_grad = (hidden_grad * lift_pre * sig * (1.0 + gate_pre * (1.0 - sig))).astype(BF16)
    lift_grad = (hidden_grad * activated).astype(BF16)
    key_gate = (key32 * rate[:, 0:1]).astype(BF16)
    key_lift = (key32 * rate[:, 1:2]).astype(BF16)
    hidden_rate = (hidden.astype(F32) * rate[:, 2:3]).astype(BF16)
    pairs = ((key_gate, gate_grad), (key_lift, lift_grad), (hidden_rate, value))
    for i, (left, right) in enumerate(pairs):
        delta_ref[i * size : (i + 1) * size, :] = lax.dot_general(
            left, right, (((0,), (0,)), ((), ())), preferred_element_type=F32
        )
    for k in range(n):
        pack(delta_ref[pl.ds(pl.multiple_of((me ^ k) * part, part), part), :], outs[k])


def update(kvr, weights, n, head, size, fresh):
    flat = [a for group in kvr for a in group]
    total = 3 * size
    rows = packing(total // n, size)[2]
    outs = [jax.ShapeDtypeStruct((rows, LANES), F32)] + [
        jax.ShapeDtypeStruct((rows, LANES), BF16)
    ] * (n - 1)
    if fresh:
        outs.append(outs[0])
    args = flat + list(weights)
    tokens = sum(g[2].shape[0] for g in kvr)
    return pl.pallas_call(
        functools.partial(update_body, n, head, size, len(kvr), fresh),
        out_shape=outs,
        in_specs=[VMEM] * len(args),
        out_specs=[VMEM] * len(outs),
        scratch_shapes=[pltpu.VMEM((total, size), BF16), pltpu.VMEM((total, size), F32)],
        compiler_params=params(-(-64 * tokens * size // MB)),
        cost_estimate=cost(2e9 * tokens / 384, 4e6),
        name="update",
    )(*args)


def renorm_body(n, part, size, *refs):
    old_ref, round_ref = refs[n : n + 2]
    full, half, _ = packing(part, size)
    delta = refs[0][...]
    for ref in refs[1:n]:
        delta = delta + ref[...].astype(F32)
    old = old_ref[...]
    summed = old + delta
    upper = lax.broadcasted_iota(jnp.int32, (half, LANES), 1) < LANES // 2 if half else None

    def row_scale(field):
        square = field * field
        total = sum(
            jnp.sum(square[j * part : (j + 1) * part], axis=-1, keepdims=True) for j in range(full)
        )
        if half:
            tail = square[full * part :]
            high = jnp.sum(jnp.where(upper, tail, 0.0), axis=-1, keepdims=True)
            low = jnp.sum(jnp.where(upper, 0.0, tail), axis=-1, keepdims=True)
            total = total + jnp.concatenate([high, low[: part - half]], axis=0)
        return total / size + epsilon

    factor = jnp.sqrt(row_scale(old)) * lax.rsqrt(row_scale(summed))
    news = [summed[j * part : (j + 1) * part] * factor for j in range(full)]
    if half:
        both = jnp.where(upper, factor[:half], lower_rows(factor[half:], half))
        news.append(summed[full * part :] * both)
    new = jnp.concatenate(news, axis=0)
    round_ref[...] = new.astype(BF16)
    if len(refs) > n + 2:
        refs[n + 2][...] = new


def renorm(parts, old, part, size, keep):
    args = list(parts) + [old]
    outs = [jax.ShapeDtypeStruct(old.shape, BF16)]
    if keep:
        outs.append(jax.ShapeDtypeStruct(old.shape, F32))
    return pl.pallas_call(
        functools.partial(renorm_body, len(parts), part, size),
        out_shape=outs,
        in_specs=[VMEM] * len(args),
        out_specs=[VMEM] * len(outs),
        compiler_params=params(4),
        cost_estimate=cost(1e6, 2e6),
        name="renorm",
    )(*args)


def head_gain(gain_ref, head, size):
    return gain_ref[...].reshape(1, -1)[:, head * size : (head + 1) * size]


def fast_rows(query, full_ref, size, gain):
    gate = full_ref[:size, :]
    lift = full_ref[size : 2 * size, :]
    down = full_ref[2 * size :, :]
    query_gate = jnp.dot(query, gate, preferred_element_type=F32)
    query_lift = jnp.dot(query, lift, preferred_element_type=F32)
    hidden = (query_gate * jax.nn.sigmoid(query_gate) * query_lift).astype(BF16)
    fast = jnp.dot(hidden, down, preferred_element_type=F32)
    return (rms(fast) * gain).astype(BF16)


def answer_body(n, head, chunks, *refs):
    me = lax.axis_index("tokens").astype(jnp.int32)
    queries = refs[:chunks]
    weights = refs[chunks : chunks + n]
    gain_ref, out_ref, full_ref = refs[chunks + n :]
    size = full_ref.shape[1]
    stack_rows(weights, full_ref, me, full_ref.shape[0] // n)
    out_ref[...] = fast_rows(
        joined(queries, head), full_ref, size, head_gain(gain_ref, head, size)
    )


def answer(queries, weights, gain, n, head, size):
    tokens = sum(q.shape[1] for q in queries)
    args = list(queries) + list(weights) + [gain]
    return pl.pallas_call(
        functools.partial(answer_body, n, head, len(queries)),
        out_shape=jax.ShapeDtypeStruct((tokens, size), BF16),
        in_specs=[VMEM] * len(args),
        out_specs=VMEM,
        scratch_shapes=[pltpu.VMEM((3 * size, size), BF16)],
        compiler_params=params(-(-64 * tokens * size // MB)),
        cost_estimate=cost(1e9 * tokens / 384, 2e6),
        name="answer",
    )(*args)


def finish_body(n, head, chunks, places, block, others, chained, *refs):
    me = lax.axis_index("tokens").astype(jnp.int32)
    origin = sources()
    queries = refs[:chunks]
    refs = refs[chunks:]
    weights = refs[:n]
    gain_ref = refs[n]
    before = refs[n + 1 : n + 1 + others]
    refs = refs[n + 1 + others + (1 if chained else 0) :]
    out_ref, full_ref, rows_ref, sem = refs
    size = full_ref.shape[1]
    stack_rows(weights, full_ref, me, full_ref.shape[0] // n)
    piece = rows_ref.shape[0] // places
    query = joined(queries, head)
    gain = head_gain(gain_ref, head, size)
    step = places // 2
    copies = []
    for first in range(0, places, step):
        rows = slice(first * piece, (first + step) * piece)
        normed = fast_rows(query[rows], full_ref, size, gain)
        wide = jnp.concatenate([ref[rows, :] for ref in before] + [normed], axis=1)
        rows_ref[rows, :] = wide
        for place in range(first, first + step):
            at = pl.multiple_of(origin[place] * piece, piece)
            copies.append(
                pltpu.make_async_copy(
                    rows_ref.at[place * piece : (place + 1) * piece],
                    out_ref.at[block, pl.ds(at, piece)],
                    sem.at[place],
                )
            )
            copies[-1].start()
    for copy in copies:
        copy.wait()


def finish(queries, weights, gain, n, head, size, others, places, block, blocks, before):
    tokens = sum(q.shape[1] for q in queries)
    width = size * (len(others) + 1)
    args = list(queries) + list(weights) + [gain] + list(others)
    specs = [VMEM] * len(args)
    alias = {}
    if before is not None:
        alias = {len(args): 0}
        args.append(before)
        specs.append(pl.BlockSpec(memory_space=pl.ANY))
    return pl.pallas_call(
        functools.partial(
            finish_body, n, head, len(queries), places, block, len(others), before is not None
        ),
        out_shape=jax.ShapeDtypeStruct((blocks, tokens, width), BF16),
        in_specs=specs,
        out_specs=pl.BlockSpec(memory_space=pl.ANY),
        scratch_shapes=[
            pltpu.VMEM((3 * size, size), BF16),
            pltpu.VMEM((tokens, width), BF16),
            pltpu.SemaphoreType.DMA((places,)),
        ],
        input_output_aliases=alias,
        compiler_params=params(-(-64 * tokens * size // MB)),
        cost_estimate=cost(1e9 * tokens / 384, 2e6),
        name="finish",
    )(*args)


def chips(pairs):
    return [(2 * a + c, 2 * b + c) for a, b in pairs for c in (0, 1)]


def shift(array, pairs):
    return lax.ppermute(array, "tensor", pairs)


def gather(rows):
    n = lax.axis_size("tensor")
    side = [(t, t ^ 1) for t in range(n)]
    outer = n // 2
    if outer == 4:
        first = shift(rows, chips([(1, 0), (3, 1), (0, 2), (2, 3)]))
        ends = shift(first, chips([(1, 0), (2, 3)]))
        mids = shift(rows, chips([(1, 2), (2, 1)]))
        last = shift(rows, chips([(2, 0), (0, 1), (3, 2), (1, 3)]))
        second = add(ends, mids)
        got = [rows, first, last, second]
    else:
        got = [rows] + [
            shift(rows, chips([(z, (z + k) % outer) for z in range(outer)]))
            for k in range(1, outer)
        ]
    pieces = []
    for piece in got:
        pieces += [piece, shift(piece, side)]
    return pieces


def sources():
    n = lax.axis_size("tensor")
    mine = lax.axis_index("tensor").astype(jnp.int32)
    outer = n // 2
    chip, core = mine // 2, mine % 2
    if outer == 4:
        high, low = chip // 2, chip % 2
        first = jnp.where(high == 0, 1 + 2 * low, 2 * low)
        last = jnp.where(high == 0, 2 - 2 * low, 3 - 2 * low)
        chip_of = [chip, first, last, 3 - chip]
    else:
        chip_of = [(chip + outer - k) % outer for k in range(outer)]
    found = []
    for c in chip_of:
        found += [c * 2 + core, c * 2 + (1 - core)]
    return found


def swap(array, k):
    n = lax.axis_size("tokens")
    return lax.ppermute(array, "tokens", [(t, t ^ k) for t in range(n)])


def local(codes, scales, w_qkv, w_rate, rate_bias, fast_gate, fast_lift, fast_down, out_gain):
    blocks = codes.shape[0]
    heads, size = fast_gate.shape[:2]
    n = lax.axis_size("tokens")
    tokens = codes.shape[1] * lax.axis_size("tensor")
    factor = rate_base / math.sqrt(tokens * n)
    rate_rows = pick(w_rate, 3 * heads)
    w_qkv = load(w_qkv)
    fresh = [fast_gate, fast_lift, fast_down]
    state = [None] * heads
    weights = [fresh] * heads
    every = tuple(range(heads))

    rows = []
    for block in range(blocks):
        rows.append(decode(codes, scales, block))
    out = None
    for block in range(blocks):
        pieces = gather(rows[block])
        first = 2 if block else -2
        early, late = pieces[:first], pieces[-2:]
        given = (w_qkv, rate_rows, rate_bias)
        query, *group = project(early, *given, heads, size, factor, block > 0)
        groups = [group]
        if block:
            groups.append(keys(pieces[2:-2], *given, every, heads, size, factor))
        queries = [query, ask(pieces[first:], w_qkv, heads, size)]
        done = []
        for head in range(heads):
            kvr = list(groups)
            found = keys(late, *given, (head,), heads, size, factor)
            late_rates = found[2] if head == 0 else late_rates
            kvr.append((found[0], found[1], late_rates))
            deltas = update(kvr, weights[head], n, head, size, block == 0)
            if block == 0:
                state[head] = deltas[n]
            parts = [deltas[0]] + [swap(deltas[k], k) for k in range(1, n)]
            rounded, *kept = renorm(parts, state[head], 3 * size // n, size, block < blocks - 1)
            state[head] = kept[0] if kept else None
            weights[head] = [rounded] + [swap(rounded, k) for k in range(1, n)]
            if head < heads - 1:
                done.append(answer(queries, weights[head], out_gain, n, head, size))
            else:
                out = finish(
                    queries, weights[head], out_gain, n, head, size, done, len(pieces), block,
                    blocks, out,
                )
    return out


def solution(mesh):
    return jax.shard_map(
        local,
        mesh=mesh,
        in_specs=(
            P(None, ("tokens", "tensor"), None),
            P(None, ("tokens", "tensor"), None),
            P(None, "tensor"),
            P(),
            P("tensor"),
            P("tensor", None, None),
            P("tensor", None, None),
            P("tensor", None, None),
            P("tensor"),
        ),
        out_specs=P(None, "tokens", "tensor"),
        check_vma=False,
    )
```

```python
import functools
import math

import jax
import jax.numpy as jnp
from jax import lax
from jax.experimental import pallas as pl
from jax.experimental.pallas import tpu as pltpu
from jax.sharding import PartitionSpec as P


epsilon = 1e-06
rate_base = 0.15
F32 = jnp.float32
BF16 = jnp.bfloat16
MB = 1 << 20


VMEM = pl.BlockSpec(memory_space=pltpu.VMEM)


def params(limit):
    return pltpu.CompilerParams(vmem_limit_bytes=limit * MB)


def cost(flops, nbytes):
    return pl.CostEstimate(flops=int(flops), bytes_accessed=int(nbytes), transcendentals=0)


def decode_body(block, steps, codes_hbm, scales_hbm, out_ref, codes_ref, scales_ref, sem):
    cols = out_ref.shape[1] // steps
    groups = cols // 32
    copies = [
        pltpu.make_async_copy(scales_hbm.at[block], scales_ref, sem.at[steps]),
    ]
    for i in range(steps):
        part = pl.ds(i * cols, cols)
        copies.append(
            pltpu.make_async_copy(codes_hbm.at[block, :, part], codes_ref.at[:, part], sem.at[i])
        )
    for copy in copies:
        copy.start()
    lane = lax.broadcasted_iota(jnp.int32, (groups, cols), 1) // 32
    row = lax.broadcasted_iota(jnp.int32, (groups, cols), 0)
    spread = jnp.where(lane == row, 1.0, 0.0).astype(BF16)
    copies[0].wait()
    scales = scales_ref[...]
    power = jnp.left_shift(jnp.ones_like(scales), scales - 119).astype(F32) * (1.0 / 131072.0)
    power = power.astype(BF16)
    for i in range(steps):
        copies[1 + i].wait()
        factor = jnp.dot(
            power[:, i * groups : (i + 1) * groups], spread, preferred_element_type=F32
        )
        codes = codes_ref[:, i * cols : (i + 1) * cols]
        lower = codes & 127
        shifted = jnp.left_shift((lower & 7) | 8, (lower >> 3) - 1)
        whole = jnp.where(lower < 8, lower, shifted).astype(F32)
        signed = jnp.where(codes >= 128, -whole, whole)
        out_ref[:, i * cols : (i + 1) * cols] = (signed * factor).astype(BF16)


def decode(codes, scales, block):
    rows, width = codes.shape[1:]
    steps = 1
    hbm = pl.BlockSpec(memory_space=pl.ANY)
    return pl.pallas_call(
        functools.partial(decode_body, block, steps),
        out_shape=jax.ShapeDtypeStruct((rows, width), BF16),
        in_specs=[hbm, hbm],
        out_specs=VMEM,
        scratch_shapes=[
            pltpu.VMEM((rows, width), jnp.int32),
            pltpu.VMEM((rows, scales.shape[2]), jnp.int32),
            pltpu.SemaphoreType.DMA((steps + 1,)),
        ],
        compiler_params=params(4),
        cost_estimate=cost(2e7, rows * width * 6),
        name="decode",
    )(
        pltpu.with_memory_space_constraint(codes, pltpu.HBM),
        pltpu.with_memory_space_constraint(scales, pltpu.HBM),
    )


def pick_body(rows_ref, out_ref):
    count = out_ref.shape[0]
    first = lax.axis_index("tensor") * (rows_ref.shape[0] // lax.axis_size("tensor"))
    row = lax.broadcasted_iota(jnp.int32, (count, rows_ref.shape[0]), 0) + first
    column = lax.broadcasted_iota(jnp.int32, (count, rows_ref.shape[0]), 1)
    hot = jnp.where(row == column, 1.0, 0.0).astype(BF16)
    out_ref[...] = jnp.dot(hot, rows_ref[...], preferred_element_type=F32).astype(BF16)


def pick(w_rate, lanes):
    count = -(-lanes // 16) * 16
    return pl.pallas_call(
        pick_body,
        out_shape=jax.ShapeDtypeStruct((count, w_rate.shape[0]), BF16),
        in_specs=[VMEM],
        out_specs=VMEM,
        compiler_params=params(4),
        name="pick",
    )(w_rate.T)


def load_body(from_ref, out_ref, sem):
    copy = pltpu.make_async_copy(from_ref, out_ref, sem)
    copy.start()
    copy.wait()


def load(array):
    return pl.pallas_call(
        load_body,
        out_shape=jax.ShapeDtypeStruct(array.shape, array.dtype),
        in_specs=[pl.BlockSpec(memory_space=pl.ANY)],
        out_specs=VMEM,
        scratch_shapes=[pltpu.SemaphoreType.DMA],
        compiler_params=params(6),
        cost_estimate=cost(0, 2 * array.size),
        name="load",
    )(pltpu.with_memory_space_constraint(array, pltpu.HBM))


def add_body(left_ref, right_ref, out_ref):
    out_ref[...] = left_ref[...] + right_ref[...]


def add(left, right):
    return pl.pallas_call(
        add_body,
        out_shape=jax.ShapeDtypeStruct(left.shape, left.dtype),
        in_specs=[VMEM] * 2,
        out_specs=VMEM,
        compiler_params=params(4),
        name="add",
    )(left, right)


LANES = 128


def joined(refs):
    return jnp.concatenate([ref[...] for ref in refs], axis=0)


def rms(field):
    return field * lax.rsqrt(jnp.mean(field * field, axis=-1, keepdims=True) + epsilon)


def rates_of(rows, w_rate_ref, bias_ref, rate_refs, factor):
    logits = lax.dot_general(
        rows, w_rate_ref[...], (((1,), (1,)), ((), ())), preferred_element_type=F32
    )
    lanes = 3 * len(rate_refs)
    rates = jax.nn.softplus(logits[:, :lanes] + bias_ref[...].reshape(1, lanes)) * factor
    for head, ref in enumerate(rate_refs):
        ref[...] = rates[:, 3 * head : 3 * head + 3]


def unit_rows(field):
    return rms(field.astype(BF16).astype(F32)).astype(BF16)


def project_body(count, heads, size, factor, blocks, *refs):
    pieces = refs[:count]
    w_ref, w_rate_ref, bias_ref = refs[count : count + 3]
    outs, all_ref = refs[count + 3 : -1], refs[-1]
    rows = joined(pieces)
    rates_of(rows, w_rate_ref, bias_ref, outs[3 * heads :], factor)
    columns = w_ref.shape[1] // blocks

    def step(i, _):
        at = pl.ds(pl.multiple_of(i * columns, LANES), columns) if blocks > 1 else slice(None)
        all_ref[:, at] = jnp.dot(rows, w_ref[:, at], preferred_element_type=F32)
        return 0

    if blocks > 1:
        lax.fori_loop(0, blocks, step, 0)
    else:
        step(0, 0)
    for head in range(heads):
        base = 3 * size * head
        q_ref, k_ref, v_ref = outs[3 * head : 3 * head + 3]
        q_ref[...] = unit_rows(all_ref[:, base : base + size])
        k_ref[...] = unit_rows(all_ref[:, base + size : base + 2 * size])
        v_ref[...] = all_ref[:, base + 2 * size : base + 3 * size].astype(BF16)


def project(pieces, w, w_rate, bias, heads, size, factor, loop):
    rows, width = pieces[0].shape
    total = rows * len(pieces)
    columns = w.shape[1]
    blocks = 3 if loop and columns % (3 * LANES) == 0 else 1
    found = pl.pallas_call(
        functools.partial(project_body, len(pieces), heads, size, factor, blocks),
        out_shape=[jax.ShapeDtypeStruct((total, size), BF16)] * (3 * heads)
        + [jax.ShapeDtypeStruct((total, 3), F32)] * heads,
        in_specs=[VMEM] * (len(pieces) + 3),
        out_specs=[VMEM] * (4 * heads),
        scratch_shapes=[pltpu.VMEM((total, columns), F32)],
        compiler_params=params(-(-8 * total * width // MB)),
        cost_estimate=cost(2 * total * width * columns, width * columns * 2),
        name="project",
    )(*pieces, w, w_rate, bias)
    queries = found[0 : 3 * heads : 3]
    return queries, [
        (found[3 * h + 1], found[3 * h + 2], found[3 * heads + h]) for h in range(heads)
    ]


def columns_of(rows, w_ref, start, stop):
    low = start // LANES * LANES
    high = min(-(-stop // LANES) * LANES, w_ref.shape[1])
    field = jnp.dot(rows, w_ref[:, low:high], preferred_element_type=F32)
    return field[:, start - low : stop - low]


def keys_body(count, wanted, size, factor, *refs):
    rows = joined(refs[:count])
    w_ref, w_rate_ref, bias_ref = refs[count : count + 3]
    outs = refs[count + 3 :]
    for place, head in enumerate(wanted):
        base = 3 * size * head + size
        both = columns_of(rows, w_ref, base, base + 2 * size)
        k_ref, v_ref = outs[2 * place : 2 * place + 2]
        k_ref[...] = unit_rows(both[:, :size])
        v_ref[...] = both[:, size:].astype(BF16)
    if wanted[0] == 0:
        rates_of(rows, w_rate_ref, bias_ref, outs[2 * len(wanted) :], factor)


def keys(pieces, w, w_rate, bias, wanted, heads, size, factor):
    rows, width = pieces[0].shape
    total = rows * len(pieces)
    many = len(wanted)
    outs = [jax.ShapeDtypeStruct((total, size), BF16)] * (2 * many)
    if wanted[0] == 0:
        outs += [jax.ShapeDtypeStruct((total, 3), F32)] * heads
    found = pl.pallas_call(
        functools.partial(keys_body, len(pieces), wanted, size, factor),
        out_shape=outs,
        in_specs=[VMEM] * (len(pieces) + 3),
        out_specs=[VMEM] * len(outs),
        compiler_params=params(-(-8 * total * width // MB)),
        cost_estimate=cost(4 * total * width * size * many, 4 * width * size * many),
        name="keys",
    )(*pieces, w, w_rate, bias)
    pairs = [(found[2 * i], found[2 * i + 1]) for i in range(many)]
    return pairs, found[2 * many :]


def ask_body(count, size, *refs):
    rows = joined(refs[:count])
    w_ref = refs[count]
    for head, q_ref in enumerate(refs[count + 1 :]):
        base = 3 * size * head
        q_ref[...] = unit_rows(columns_of(rows, w_ref, base, base + size))


def ask(pieces, w, heads, size):
    rows, width = pieces[0].shape
    total = rows * len(pieces)
    return pl.pallas_call(
        functools.partial(ask_body, len(pieces), size),
        out_shape=[jax.ShapeDtypeStruct((total, size), BF16)] * heads,
        in_specs=[VMEM] * (len(pieces) + 1),
        out_specs=[VMEM] * heads,
        compiler_params=params(-(-8 * total * width // MB)),
        cost_estimate=cost(2 * total * width * size * heads, width * size * 4),
        name="ask",
    )(*pieces, w)


def packing(part, size):
    full, rest = divmod(size, LANES)
    if rest not in (0, LANES // 2):
        raise ValueError("head size")
    half = -(-part // 32) * 16 if rest else 0
    return full, half, full * part + half


def lower_rows(array, rows):
    missing = rows - array.shape[0]
    if not missing:
        return array
    return jnp.concatenate([array, jnp.zeros((missing, array.shape[1]), array.dtype)], axis=0)


def pack(rows, out_ref):
    part, size = rows.shape
    full, half, _ = packing(part, size)
    kind = out_ref.dtype
    for j in range(full):
        out_ref[j * part : (j + 1) * part, :] = rows[:, j * LANES : (j + 1) * LANES].astype(kind)
    if half:
        rest = rows[:, full * LANES :]
        tail = jnp.concatenate([rest[:half], lower_rows(rest[half:], half)], axis=1)
        out_ref[full * part :, :] = tail.astype(kind)


def stack_rows(refs, full_ref, me, part):
    full, half, _ = packing(part, full_ref.shape[1])
    for k, ref in enumerate(refs):
        at = pl.multiple_of((me ^ k) * part, part)
        for j in range(full):
            full_ref[pl.ds(at, part), j * LANES : (j + 1) * LANES] = ref[
                j * part : (j + 1) * part, :
            ]
        if half:
            tail = ref[full * part :, :]
            low = part - half
            full_ref[pl.ds(at, half), full * LANES :] = tail[:, : LANES // 2]
            full_ref[pl.ds(at + half, low), full * LANES :] = tail[:low, LANES // 2 :]


def update_body(n, head, size, chunks, fresh, *refs):
    me = lax.axis_index("tokens").astype(jnp.int32)
    kvr = refs[: 3 * chunks]
    refs = refs[3 * chunks :]
    many = 3 if fresh else n
    weights = refs[:many]
    refs = refs[many:]
    outs = refs[:n]
    full_ref, delta_ref = refs[-2:]
    part = full_ref.shape[0] // n
    if fresh:
        for i in range(3):
            matrix = weights[i][head]
            full_ref[i * size : (i + 1) * size, :] = matrix.astype(BF16)
            delta_ref[i * size : (i + 1) * size, :] = matrix
        pack(delta_ref[pl.ds(pl.multiple_of(me * part, part), part), :], refs[n])
    else:
        stack_rows(weights, full_ref, me, part)
    gate = full_ref[:size, :]
    lift = full_ref[size : 2 * size, :]
    down = full_ref[2 * size :, :]
    key = joined(kvr[0::3])
    value = joined(kvr[1::3])
    rate = joined(kvr[2::3])
    key32 = key.astype(F32)
    gate_pre = jnp.dot(key, gate, preferred_element_type=F32)
    lift_pre = jnp.dot(key, lift, preferred_element_type=F32)
    hidden_grad = lax.dot_general(
        value, down, (((1,), (1,)), ((), ())), preferred_element_type=F32
    )
    sig = jax.nn.sigmoid(gate_pre)
    activated = gate_pre * sig
    hidden = (activated * lift_pre).astype(BF16)
    gate_grad = (hidden_grad * lift_pre * sig * (1.0 + gate_pre * (1.0 - sig))).astype(BF16)
    lift_grad = (hidden_grad * activated).astype(BF16)
    key_gate = (key32 * rate[:, 0:1]).astype(BF16)
    key_lift = (key32 * rate[:, 1:2]).astype(BF16)
    hidden_rate = (hidden.astype(F32) * rate[:, 2:3]).astype(BF16)
    pairs = ((key_gate, gate_grad), (key_lift, lift_grad), (hidden_rate, value))
    for i, (left, right) in enumerate(pairs):
        delta_ref[i * size : (i + 1) * size, :] = lax.dot_general(
            left, right, (((0,), (0,)), ((), ())), preferred_element_type=F32
        )
    for k in range(n):
        pack(delta_ref[pl.ds(pl.multiple_of((me ^ k) * part, part), part), :], outs[k])


def update(kvr, weights, n, head, size, fresh):
    flat = [a for group in kvr for a in group]
    total = 3 * size
    rows = packing(total // n, size)[2]
    outs = [jax.ShapeDtypeStruct((rows, LANES), F32)] + [
        jax.ShapeDtypeStruct((rows, LANES), BF16)
    ] * (n - 1)
    if fresh:
        outs.append(outs[0])
    args = flat + list(weights)
    tokens = sum(group[2].shape[0] for group in kvr)
    return pl.pallas_call(
        functools.partial(update_body, n, head if fresh else 0, size, len(kvr), fresh),
        out_shape=outs,
        in_specs=[VMEM] * len(args),
        out_specs=[VMEM] * len(outs),
        scratch_shapes=[pltpu.VMEM((total, size), BF16), pltpu.VMEM((total, size), F32)],
        compiler_params=params(-(-64 * tokens * size // MB)),
        cost_estimate=cost(2e9 * tokens / 384, 4e6),
        name="update",
    )(*args)


def renorm_body(n, part, size, *refs):
    old_ref, round_ref = refs[n : n + 2]
    full, half, _ = packing(part, size)
    delta = refs[0][...]
    for ref in refs[1:n]:
        delta = delta + ref[...].astype(F32)
    old = old_ref[...]
    summed = old + delta
    upper = lax.broadcasted_iota(jnp.int32, (half, LANES), 1) < LANES // 2 if half else None

    def row_scale(field):
        square = field * field
        total = sum(
            jnp.sum(square[j * part : (j + 1) * part], axis=-1, keepdims=True) for j in range(full)
        )
        if half:
            tail = square[full * part :]
            high = jnp.sum(jnp.where(upper, tail, 0.0), axis=-1, keepdims=True)
            low = jnp.sum(jnp.where(upper, 0.0, tail), axis=-1, keepdims=True)
            total = total + jnp.concatenate([high, low[: part - half]], axis=0)
        return total / size + epsilon

    factor = jnp.sqrt(row_scale(old)) * lax.rsqrt(row_scale(summed))
    news = [summed[j * part : (j + 1) * part] * factor for j in range(full)]
    if half:
        both = jnp.where(upper, factor[:half], lower_rows(factor[half:], half))
        news.append(summed[full * part :] * both)
    new = jnp.concatenate(news, axis=0)
    round_ref[...] = new.astype(BF16)
    if len(refs) > n + 2:
        refs[n + 2][...] = new


def renorm(parts, old, part, size, keep):
    args = list(parts) + [old]
    outs = [jax.ShapeDtypeStruct(old.shape, BF16)]
    if keep:
        outs.append(jax.ShapeDtypeStruct(old.shape, F32))
    return pl.pallas_call(
        functools.partial(renorm_body, len(parts), part, size),
        out_shape=outs,
        in_specs=[VMEM] * len(args),
        out_specs=[VMEM] * len(outs),
        compiler_params=params(4),
        cost_estimate=cost(1e6, 2e6),
        name="renorm",
    )(*args)


def head_gain(gain_ref, head, size):
    return gain_ref[...].reshape(1, -1)[:, head * size : (head + 1) * size]


def fast_rows(query, full_ref, size, gain):
    gate = full_ref[:size, :]
    lift = full_ref[size : 2 * size, :]
    down = full_ref[2 * size :, :]
    query_gate = jnp.dot(query, gate, preferred_element_type=F32)
    query_lift = jnp.dot(query, lift, preferred_element_type=F32)
    hidden = (query_gate * jax.nn.sigmoid(query_gate) * query_lift).astype(BF16)
    fast = jnp.dot(hidden, down, preferred_element_type=F32)
    return (rms(fast) * gain).astype(BF16)


def answer_body(n, head, chunks, *refs):
    me = lax.axis_index("tokens").astype(jnp.int32)
    queries = refs[:chunks]
    weights = refs[chunks : chunks + n]
    gain_ref, out_ref, full_ref = refs[chunks + n :]
    size = full_ref.shape[1]
    stack_rows(weights, full_ref, me, full_ref.shape[0] // n)
    out_ref[...] = fast_rows(
        joined(queries), full_ref, size, head_gain(gain_ref, head, size)
    )


def answer(queries, weights, gain, n, head, size):
    tokens = sum(q.shape[0] for q in queries)
    args = list(queries) + list(weights) + [gain]
    return pl.pallas_call(
        functools.partial(answer_body, n, head, len(queries)),
        out_shape=jax.ShapeDtypeStruct((tokens, size), BF16),
        in_specs=[VMEM] * len(args),
        out_specs=VMEM,
        scratch_shapes=[pltpu.VMEM((3 * size, size), BF16)],
        compiler_params=params(-(-64 * tokens * size // MB)),
        cost_estimate=cost(1e9 * tokens / 384, 2e6),
        name="answer",
    )(*args)


def finish_body(n, head, chunks, places, block, others, chained, *refs):
    me = lax.axis_index("tokens").astype(jnp.int32)
    origin = sources()
    queries = refs[:chunks]
    refs = refs[chunks:]
    weights = refs[:n]
    gain_ref = refs[n]
    before = refs[n + 1 : n + 1 + others]
    refs = refs[n + 1 + others + (1 if chained else 0) :]
    out_ref, full_ref, rows_ref, sem = refs
    size = full_ref.shape[1]
    stack_rows(weights, full_ref, me, full_ref.shape[0] // n)
    piece = rows_ref.shape[0] // places
    query = joined(queries)
    gain = head_gain(gain_ref, head, size)
    normed = fast_rows(query, full_ref, size, gain)
    rows_ref[...] = jnp.concatenate([ref[...] for ref in before] + [normed], axis=1)
    copies = []
    for place in range(places):
        at = pl.multiple_of(origin[place] * piece, piece)
        copies.append(
            pltpu.make_async_copy(
                rows_ref.at[place * piece : (place + 1) * piece],
                out_ref.at[block, pl.ds(at, piece)],
                sem.at[place],
            )
        )
        copies[-1].start()
    for copy in copies:
        copy.wait()


def finish(queries, weights, gain, n, head, size, others, places, block, blocks, before):
    tokens = sum(q.shape[0] for q in queries)
    width = size * (len(others) + 1)
    args = list(queries) + list(weights) + [gain] + list(others)
    specs = [VMEM] * len(args)
    alias = {}
    if before is not None:
        alias = {len(args): 0}
        args.append(before)
        specs.append(pl.BlockSpec(memory_space=pl.ANY))
    return pl.pallas_call(
        functools.partial(
            finish_body, n, head, len(queries), places, block, len(others), before is not None
        ),
        out_shape=jax.ShapeDtypeStruct((blocks, tokens, width), BF16),
        in_specs=specs,
        out_specs=pl.BlockSpec(memory_space=pl.ANY),
        scratch_shapes=[
            pltpu.VMEM((3 * size, size), BF16),
            pltpu.VMEM((tokens, width), BF16),
            pltpu.SemaphoreType.DMA((places,)),
        ],
        input_output_aliases=alias,
        compiler_params=params(-(-64 * tokens * size // MB)),
        cost_estimate=cost(1e9 * tokens / 384, 2e6),
        name="finish",
    )(*args)


def chips(pairs):
    return [(2 * a + c, 2 * b + c) for a, b in pairs for c in (0, 1)]


def shift(array, pairs):
    return lax.ppermute(array, "tensor", pairs)


def gather(rows):
    n = lax.axis_size("tensor")
    side = [(t, t ^ 1) for t in range(n)]
    outer = n // 2
    if outer == 4:
        first = shift(rows, chips([(1, 0), (3, 1), (0, 2), (2, 3)]))
        ends = shift(first, chips([(1, 0), (2, 3)]))
        mids = shift(rows, chips([(1, 2), (2, 1)]))
        last = shift(rows, chips([(2, 0), (0, 1), (3, 2), (1, 3)]))
        second = add(ends, mids)
        got = [rows, first, last, second]
    else:
        got = [rows] + [
            shift(rows, chips([(z, (z + k) % outer) for z in range(outer)]))
            for k in range(1, outer)
        ]
    pieces = []
    for piece in got:
        pieces += [piece, shift(piece, side)]
    return pieces


def sources():
    n = lax.axis_size("tensor")
    mine = lax.axis_index("tensor").astype(jnp.int32)
    outer = n // 2
    chip, core = mine // 2, mine % 2
    if outer == 4:
        high, low = chip // 2, chip % 2
        first = jnp.where(high == 0, 1 + 2 * low, 2 * low)
        last = jnp.where(high == 0, 2 - 2 * low, 3 - 2 * low)
        chip_of = [chip, first, last, 3 - chip]
    else:
        chip_of = [(chip + outer - k) % outer for k in range(outer)]
    found = []
    for c in chip_of:
        found += [c * 2 + core, c * 2 + (1 - core)]
    return found


def swap(array, k):
    n = lax.axis_size("tokens")
    return lax.ppermute(array, "tokens", [(t, t ^ k) for t in range(n)])


def local(codes, scales, w_qkv, w_rate, rate_bias, fast_gate, fast_lift, fast_down, out_gain):
    blocks = codes.shape[0]
    heads, size = fast_gate.shape[:2]
    n = lax.axis_size("tokens")
    tokens = codes.shape[1] * lax.axis_size("tensor")
    factor = rate_base / math.sqrt(tokens * n)
    rate_rows = pick(w_rate, 3 * heads)
    w_qkv = load(w_qkv)
    fresh = [fast_gate, fast_lift, fast_down]
    state = [None] * heads
    weights = [fresh] * heads
    every = tuple(range(heads))

    rows = []
    for block in range(blocks):
        rows.append(decode(codes, scales, block))
    out = None
    for block in range(blocks):
        pieces = gather(rows[block])
        final = block == blocks - 1
        first = 2 if block else 4
        early, late = pieces[:first], pieces[-2:]
        given = (w_qkv, rate_rows, rate_bias)
        asked, ready = project(early, *given, heads, size, factor, True)
        middle = keys(pieces[first:-2], *given, every, heads, size, factor)
        if not final:
            last = keys(late, *given, every, heads, size, factor)
        more = ask(pieces[first:], w_qkv, heads, size)
        done = []
        for head in range(heads):
            queries = [asked[head], more[head]]
            if final:
                pairs, rates = keys(late, *given, (head,), heads, size, factor)
                late_rates = rates or late_rates
                final_pair = pairs[0]
            else:
                final_pair, late_rates = last[0][head], last[1]
            kvr = [
                ready[head],
                (*middle[0][head], middle[1][head]),
                (*final_pair, late_rates[head]),
            ]
            deltas = update(kvr, weights[head], n, head, size, block == 0)
            if block == 0:
                state[head] = deltas[n]
            parts = [deltas[0]] + [swap(deltas[k], k) for k in range(1, n)]
            rounded, *kept = renorm(parts, state[head], 3 * size // n, size, block < blocks - 1)
            state[head] = kept[0] if kept else None
            weights[head] = [rounded] + [swap(rounded, k) for k in range(1, n)]
            if head < heads - 1:
                done.append(answer(queries, weights[head], out_gain, n, head, size))
            else:
                out = finish(
                    queries, weights[head], out_gain, n, head, size, done, len(pieces), block,
                    blocks, out,
                )
    return out


def solution(mesh):
    return jax.shard_map(
        local,
        mesh=mesh,
        in_specs=(
            P(None, ("tokens", "tensor"), None),
            P(None, ("tokens", "tensor"), None),
            P(None, "tensor"),
            P(),
            P("tensor"),
            P("tensor", None, None),
            P("tensor", None, None),
            P("tensor", None, None),
            P("tensor"),
        ),
        out_specs=P(None, "tokens", "tensor"),
        check_vma=False,
    )
```
